256 devices in a mesh: gx: 8 (over x, core), gy: 4 (over y), gz: 8 (over z).
Axes of the slice: x: 4, y: 4, z: 8, core: 2. Of those that a mesh axis runs over, the one named last changes fastest.
Arguments:
- t_matrix: float32 [1, 8, 4, 32, 1024], P(None, 'gx', 'gy', 'gz'), may hold values from -3 to 3
- structure: float32 [1, 1440, 1440], replicated, may hold values from -0.0390625 to 0.0390625
- species: int32 [8, 4, 32], P('gx', 'gy', 'gz'), may hold values from 0 to 3
- members: int32 [8, 4, 32, 45], P('gx', 'gy', 'gz'), may hold values from -1 to 44, as said below
- delta_table: float32 [4, 1024], replicated, may hold values from -4 to 4
Outputs:
- site_tau: float32 [1, 8, 4, 32, 1024], P(None, 'gx', 'gy', 'gz')
- pair_terms: float32 [8, 4, 32, 45], P('gx', 'gy', 'gz')
The draws below stay inside these ranges and needn't reach their ends.
Inputs may be any that keep to these rules, and one draw needn't show every extreme that they name: `members`: each site's list names distinct window cells, the centre cell first, 27 to 45 of them, then -1 in the remaining slots; in every draw some site lists all 45 cells.
All inputs are finite; a program needn't handle non-finite values.
Results may differ from the reference program's by a relative error of at most 0.00013.
Values sent between devices are 32-bit elements; how exact they have to be, the bound alone decides.
A program may use at most 192 MiB of HBM per device.

```python
import jax
import jax.numpy as jnp
from jax import lax

L2 = 32
WINDOW = 45
ITERS = 4
ENERGIES = 1
SPECIES = 4
NX = 8
NY = 4
NZ = 32


def draw_members(key, part):
    window_cells = jnp.arange(WINDOW, dtype=jnp.int32)
    score_key = jax.random.fold_in(key, 11)
    count_key = jax.random.fold_in(key, 23)
    scores = jax.random.randint(score_key, (NX, NY, NZ, WINDOW), 0, 1 << 20, dtype=jnp.int32)
    scores = scores * 64 + window_cells
    scores = jnp.where(window_cells == WINDOW // 2, -1, scores)
    ordered = jnp.argsort(scores, axis=-1, stable=True).astype(jnp.int32)
    counts = jax.random.randint(count_key, (NX * NY * NZ,), 27, WINDOW + 1, dtype=jnp.int32)
    counts = counts.at[0].set(WINDOW).reshape(NX, NY, NZ, 1)
    return jnp.where(window_cells < counts, ordered, -1).astype(jnp.int32)


def with_ends(drawn, key, least, largest):
    spot = [jax.random.randint(jax.random.fold_in(key, axis), (), 0, length) for axis, length in enumerate(drawn.shape)]
    widest = drawn.shape.index(max(drawn.shape))
    neighbour = spot[:widest] + [(spot[widest] + 1) % drawn.shape[widest]] + spot[widest + 1:]
    return drawn.at[tuple(spot)].set(least).at[tuple(neighbour)].set(largest)


def shard_levels(key, dims, cuts, least, top_value):
    level, own = 1.0, jax.random.fold_in(key, 6)
    for position, parts in cuts:
        draws = jnp.exp(jax.random.uniform(jax.random.fold_in(own, position), (parts,), jnp.float32, least / len(cuts), top_value / len(cuts)))
        level = level * jnp.repeat(draws, dims[position] // parts).reshape([-1 if axis == position else 1 for axis in range(len(dims))])
    return level


def bell_draw(own_key, dims, spread, limit, cuts=(), kind=jnp.bfloat16):
    entries = jax.random.normal(own_key, dims, jnp.float32) * spread
    if len(cuts) > 0:
        entries = shard_levels(own_key, dims, cuts, -0.22, 0.18) * entries
    return jnp.clip(entries, min=-limit, max=limit).astype(kind)


def setup_inputs(seed: int = 0) -> dict:
    key_of = jax.random.split(jax.random.key(seed), 6)
    return {
        "t_matrix": bell_draw(key_of[0], (ENERGIES, NX, NY, NZ, L2 * L2), 0.5, 3.0, ((1, 8), (2, 4), (3, 8)), jnp.float32),
        "structure": bell_draw(key_of[1], (ENERGIES, WINDOW * L2, WINDOW * L2), (16 * WINDOW * L2) ** -0.5, 0.0390625, (), jnp.float32),
        "species": with_ends(jax.random.randint(key_of[2], (NX, NY, NZ), 0, SPECIES), jax.random.fold_in(key_of[2], 1), 0, SPECIES - 1).astype(jnp.int32),
        "members": draw_members(jax.random.fold_in(key_of[5], 71), 0),
        "delta_table": bell_draw(key_of[4], (SPECIES, L2 * L2), 0.6, 4.0, (), jnp.float32),
    }


highest = lax.Precision.HIGHEST


def cell_offset(cell_index):
    return cell_index // 15 - 1, (cell_index // 5) % 3 - 1, cell_index % 5 - 2


def reference(t_matrix, structure, species, members, delta_table):
    site_count = NX * NY * NZ
    centre = WINDOW // 2
    window_cells = jnp.arange(WINDOW, dtype=jnp.int32)
    member = jnp.any(members[..., None] == window_cells, axis=-2).astype(jnp.float32)
    member = member.reshape(site_count, WINDOW).T
    onehot = (species.reshape(site_count, 1) == jnp.arange(SPECIES, dtype=jnp.int32)).astype(jnp.float32)
    delta_site = jnp.dot(onehot, delta_table, precision=highest, preferred_element_type=jnp.float32)
    delta_site = delta_site.reshape(site_count, L2, L2)
    tau_list = []
    pair_sums = jnp.zeros((WINDOW, site_count), jnp.float32)
    for energy in range(ENERGIES):
        site_matrices = t_matrix[energy].reshape(NX, NY, NZ, L2, L2)
        shifted = []
        for cell_index in range(WINDOW):
            shift_x, shift_y, shift_z = cell_offset(cell_index)
            rolled = jnp.roll(site_matrices, (-shift_x, -shift_y, -shift_z), axis=(0, 1, 2))
            shifted.append(rolled.reshape(site_count, L2, L2))
        window_matrices = jnp.stack(shifted)
        own_rows = jnp.transpose(site_matrices.reshape(site_count, L2, L2), (1, 0, 2))
        start_column = jnp.zeros((WINDOW, L2, site_count, L2), jnp.float32).at[centre].set(own_rows)
        column = start_column
        for sweep_index in range(ITERS):
            image_rows = jnp.dot(structure[energy], column.reshape(WINDOW * L2, site_count * L2),
                                 precision=highest, preferred_element_type=jnp.float32)
            image_rows = image_rows.reshape(WINDOW, L2, site_count, L2)
            moved_rows = jnp.einsum('psab,pbsc->pasc', window_matrices, image_rows, precision=highest)
            column = start_column + member[:, None, :, None] * moved_rows
        tau_list.append(jnp.transpose(column[centre], (1, 0, 2)).reshape(NX, NY, NZ, L2 * L2))
        right_blocks = jnp.einsum('carb,rbd->crad', column, delta_site, precision=highest)
        right_grid = right_blocks.reshape(WINDOW, NX, NY, NZ, L2, L2)
        terms = []
        for cell_index in range(WINDOW):
            shift_x, shift_y, shift_z = cell_offset(cell_index)
            incoming = jnp.roll(right_grid[WINDOW - 1 - cell_index], (-shift_x, -shift_y, -shift_z), axis=(0, 1, 2))
            incoming = incoming.reshape(site_count, L2, L2)
            left_blocks = jnp.einsum('sab,sbd->sad', delta_site, incoming, precision=highest)
            terms.append(jnp.einsum('sad,dsa->s', left_blocks, column[cell_index], precision=highest))
        pair_sums = pair_sums + jnp.stack(terms)
    site_tau = jnp.stack(tau_list)
    pair_terms = pair_sums.T.reshape(NX, NY, NZ, WINDOW)
    return site_tau, pair_terms
```

```python
import jax
import jax.numpy as jnp
from jax import lax
from jax.experimental import pallas as pl
from jax.experimental.pallas import tpu as pltpu
from jax.sharding import PartitionSpec as P

L2 = 32
WINDOW = 45
ITERS = 4
SPECIES = 4
DEPTH = 4
LANES = DEPTH * L2
ROWS = WINDOW * L2
PADDED = 1536
CHUNK = ROWS // 3
CELLS = WINDOW // 3
CENTRE = WINDOW // 2
F32 = jnp.float32
BF16 = jnp.bfloat16
MESH = pl.DeviceIdType.MESH


def split(x):
    high = x.astype(BF16)
    return high, (x - high.astype(F32)).astype(BF16)


def dot(a, b):
    return jnp.dot(a, b, preferred_element_type=F32)


def kernel(
    t_ref,
    s_hbm,
    species_ref,
    members_ref,
    dtab_ref,
    tau_ref,
    pair_ref,
    sf,
    sh,
    sl,
    w,
    tw,
    halo_c,
    halo_l,
    halo_r,
    pack_u,
    pack_d,
    mask,
    blocks,
    dbd,
    rnat,
    rb,
    prow,
    msend,
    usend,
    dsend,
    mrecv,
    urecv,
    drecv,
    s_sem,
    hc_send,
    hl_send,
    hr_send,
    hc_recv,
    hl_recv,
    hr_recv,
    m_send,
    u_send,
    d_send,
    m_recv,
    u_recv,
    d_recv,
):
    gx, gy, gz = lax.axis_index("gx"), lax.axis_index("gy"), lax.axis_index("gz")
    nx, ny, nz = lax.axis_size("gx"), lax.axis_size("gy"), lax.axis_size("gz")

    def peer(dx, dy, dz):
        return (
            lax.rem(gx + dx + nx, nx),
            lax.rem(gy + dy + ny, ny),
            lax.rem(gz + dz + nz, nz),
        )

    def rows_copy(i):
        rows = pl.ds(pl.multiple_of(i * 160, 160), 160)
        return pltpu.make_async_copy(s_hbm.at[0, rows, :], sf.at[rows, :], s_sem.at[i])

    @pl.loop(0, 9)
    def _(i):
        rows_copy(i).start()

    barrier = pltpu.get_barrier_semaphore()

    @pl.loop(0, 27)
    def _(n):
        @pl.when(n != 13)
        def _():
            pl.semaphore_signal(
                barrier,
                inc=1,
                device_id=peer(n // 9 - 1, lax.rem(n // 3, 3) - 1, lax.rem(n, 3) - 1),
                device_id_type=MESH,
            )

    lane = lax.broadcasted_iota(jnp.int32, (L2, LANES), 1)
    lane16 = lax.broadcasted_iota(jnp.int32, (L2 // 2, LANES), 1)
    t = t_ref[...]
    top, low = t[: L2 // 2], t[L2 // 2 :]
    pack_u[...] = jnp.where(lane16 < 64, pltpu.roll(top, 64, 1), low)
    pack_d[...] = jnp.where(lane16 < 64, top, pltpu.roll(low, 64, 1))
    halo_c[4] = t

    pl.semaphore_wait(barrier, 26)

    def remote(src, dst, send, recv, device):
        return pltpu.make_async_remote_copy(
            src_ref=src,
            dst_ref=dst,
            send_sem=send,
            recv_sem=recv,
            device_id=device,
            device_id_type=MESH,
        )

    def halo(plane):
        dx, dy = plane // 3 - 1, lax.rem(plane, 3) - 1
        slot = 8 - plane
        c = remote(t_ref, halo_c.at[slot], hc_send.at[plane], hc_recv.at[slot], peer(dx, dy, 0))
        u = remote(pack_u, halo_l.at[slot], hl_send.at[plane], hl_recv.at[slot], peer(dx, dy, 1))
        d = remote(pack_d, halo_r.at[slot], hr_send.at[plane], hr_recv.at[slot], peer(dx, dy, -1))
        return c, u, d

    @pl.loop(0, 9)
    def _(plane):
        c, u, d = halo(plane)

        @pl.when(plane != 4)
        def _():
            c.start()

        u.start()
        d.start()

    cells = lax.broadcasted_iota(jnp.int32, (48, WINDOW), 0)
    lane48 = lax.broadcasted_iota(jnp.int32, (48, LANES), 1)
    member = jnp.zeros((48, LANES), F32)
    for s in range(DEPTH):
        hit = jnp.where(members_ref[s : s + 1, :] == cells, 1.0, 0.0).astype(F32)
        some = jnp.max(hit, axis=1, keepdims=True)
        member = jnp.where(lane48 // L2 == s, some, member)
    mask[...] = member

    br = lax.broadcasted_iota(jnp.int32, (LANES, LANES), 0)
    bc = lax.broadcasted_iota(jnp.int32, (LANES, LANES), 1)
    blocks[...] = jnp.where(br // L2 == bc // L2, 1.0, 0.0).astype(BF16)

    for s in range(DEPTH):
        own = dtab_ref[0]
        for k in range(1, SPECIES):
            own = jnp.where(species_ref[s] == k, dtab_ref[k], own)
        dh, dl = split(jnp.where(lane // L2 == s, own, 0.0))
        rows = slice(s * L2, (s + 1) * L2)
        down = slice(LANES + s * L2, LANES + (s + 1) * L2)
        dbd[rows, :LANES] = dh
        dbd[rows, LANES:] = dl
        dbd[down, :LANES] = dh
        dbd[down, LANES:] = jnp.zeros((L2, LANES), BF16)

    w[:, 512:768, :] = jnp.zeros((2, 256, 2 * LANES), BF16)
    w[:, ROWS:, :] = jnp.zeros((2, PADDED - ROWS, 2 * LANES), BF16)
    th, tl = split(t)
    w[0, CENTRE * L2 : (CENTRE + 1) * L2, :LANES] = th
    w[0, CENTRE * L2 : (CENTRE + 1) * L2, LANES:] = tl
    sh[:, ROWS:] = jnp.zeros((ROWS, PADDED - ROWS), BF16)
    sl[:, ROWS:] = jnp.zeros((ROWS, PADDED - ROWS), BF16)

    @pl.loop(0, 9)
    def _(i):
        rows_copy(i).wait()
        rows = pl.ds(pl.multiple_of(i * 160, 160), 160)
        high, rest = split(sf[rows, :])
        sh[rows, :ROWS] = high
        sl[rows, :ROWS] = rest

    @pl.loop(0, 9)
    def _(plane):
        c, u, d = halo(8 - plane)

        @pl.when(plane != 4)
        def _():
            c.wait_recv()

        u.wait_recv()
        d.wait_recv()
        centre = halo_c[plane]
        up, down = halo_l[plane], halo_r[plane]
        left = jnp.concatenate([pltpu.roll(up, 64, 1), up], axis=0)
        right = jnp.concatenate([down, pltpu.roll(down, 64, 1)], axis=0)
        windows = [
            pltpu.roll(jnp.where(lane < 64, centre, left), 64, 1),
            pltpu.roll(jnp.where(lane < 96, centre, left), 32, 1),
            centre,
            pltpu.roll(jnp.where(lane < 32, right, centre), 96, 1),
            pltpu.roll(jnp.where(lane < 64, right, centre), 64, 1),
        ]
        for k in range(5):
            cell = plane * 5 + k
            th, tl = split(windows[k] * mask[pl.ds(cell, 1), :])
            tw[cell, :L2] = th
            tw[cell, L2:] = tl

    def chunk(g, now, later, first=False, last=False):
        rows = pl.ds(pl.multiple_of(g * CHUNK, CHUNK), CHUNK)
        if first:
            wide = w[0, 512:768, :]
            a = dot(sh[rows, 512:768], wide)
            b = dot(sl[rows, 512:768], wide[:, :LANES])
        else:
            wide = w[now]
            a = dot(sh[rows, :], wide)
            b = dot(sl[rows, :], wide[:, :LANES])
        image = a[:, :LANES] + (a[:, LANES:] + b)
        on = blocks[...]
        columns = []
        for i in range(CELLS):
            ih, il = split(image[i * L2 : (i + 1) * L2])
            wbd = jnp.concatenate(
                [
                    jnp.concatenate([ih] * DEPTH, axis=0) * on,
                    jnp.concatenate([il] * DEPTH, axis=0) * on,
                ],
                axis=1,
            )
            res = dot(tw[g * CELLS + i], wbd)
            x = res[:L2, :LANES] + (res[:L2, LANES:] + res[L2:, :LANES])
            if i == CELLS // 2:
                x = x + t_ref[...] * jnp.where(g == 1, 1.0, 0.0).astype(F32)
                if last:

                    @pl.when(g == 1)
                    def _():
                        tau_ref[...] = x

            xh, xl = split(x)
            columns.append(jnp.concatenate([xh, xl], axis=1))
        columns = jnp.concatenate(columns, axis=0)
        if not last:
            w[later, rows, :] = columns
            return
        r2 = dot(columns, dbd[...])
        r = r2[:, :LANES] + r2[:, LANES:]
        rnat[rows, :] = r
        for j in range(3):
            turned = []
            for k in range(5):
                at = (j * 5 + k) * L2
                block = r[at : at + L2]
                turned.append(pltpu.roll(block, (L2 * (k - 2)) % LANES, 1) if k != 2 else block)
            plane = g * 3 + j
            kept = [
                turned[2],
                turned[3],
                turned[1],
                jnp.where(lane >= 64, turned[4], turned[0]),
            ]
            usend[plane] = jnp.where(lane < 64, turned[4], pltpu.roll(turned[3], 64, 1))
            dsend[plane] = jnp.where(lane >= 64, turned[0], pltpu.roll(turned[1], 64, 1))
            c, u, d = pairs(plane)
            u.start()
            d.start()

            def away():
                for n in range(4):
                    msend[plane, n] = kept[n]
                c.start()

            if j == 1:
                pl.when(g != 1)(away)

                @pl.when(g == 1)
                def _():
                    for n in range(4):
                        mrecv[4, n] = kept[n]
            else:
                away()

    def pairs(plane):
        dx, dy = plane // 3 - 1, lax.rem(plane, 3) - 1
        c = remote(msend.at[plane], mrecv.at[plane], m_send.at[plane], m_recv.at[plane], peer(dx, dy, 0))
        u = remote(usend.at[plane], urecv.at[plane], u_send.at[plane], u_recv.at[plane], peer(dx, dy, 1))
        d = remote(dsend.at[plane], drecv.at[plane], d_send.at[plane], d_recv.at[plane], peer(dx, dy, -1))
        return c, u, d

    @pl.loop(0, 3)
    def _(g):
        chunk(g, 0, 1, first=True)

    @pl.loop(0, (ITERS - 2) * 3)
    def _(n):
        now = lax.rem(n // 3 + 1, 2)
        chunk(lax.rem(n, 3), now, 1 - now)

    @pl.loop(0, 3)
    def _(n):
        chunk(lax.rem(2 * n, 3), (ITERS - 1) % 2, 0, last=True)

    rnat[ROWS:, :] = jnp.zeros((PADDED - ROWS, LANES), F32)

    @pl.loop(0, 12)
    def _(i):
        turned = rnat[pl.ds(pl.multiple_of(i * LANES, LANES), LANES), :].T
        for j in range(4):
            out = None
            for s in range(DEPTH):
                part = turned[s * L2 : (s + 1) * L2]
                shift = (L2 * (s - j)) % LANES
                part = pltpu.roll(part, shift, 1) if shift else part
                out = part if out is None else jnp.where(lane // L2 == s, part, out)
            rb[i * 4 + j] = out

    @pl.loop(0, 9)
    def _(n):
        plane = jnp.where(n == 0, 4, jnp.where(n <= 4, n - 1, n))
        c, u, d = pairs(plane)

        @pl.when(n != 0)
        def _():
            c.wait_recv()

        u.wait_recv()
        d.wait_recv()
        up, down = urecv[plane], drecv[plane]
        split_block = mrecv[plane, 3]
        got = [
            jnp.where(lane < 64, split_block, down),
            jnp.where(lane < 96, mrecv[plane, 2], pltpu.roll(down, 64, 1)),
            mrecv[plane, 0],
            jnp.where(lane < 32, pltpu.roll(up, 64, 1), mrecv[plane, 1]),
            jnp.where(lane < 64, up, split_block),
        ]
        for k in range(5):
            cell = WINDOW - 1 - (plane * 5 + k)
            prow[pl.ds(cell, 1), :] = jnp.sum(got[k] * rb[cell], axis=0, keepdims=True)

    prow[WINDOW:, :] = jnp.zeros((48 - WINDOW, LANES), F32)
    sr = lax.broadcasted_iota(jnp.int32, (8, LANES), 0)
    sc = lax.broadcasted_iota(jnp.int32, (8, LANES), 1)
    chosen = jnp.where(sc // L2 == sr, 1.0, 0.0).astype(F32)
    sums = lax.dot_general(
        chosen,
        prow[...],
        (((1,), (1,)), ((), ())),
        precision=lax.Precision.HIGHEST,
        preferred_element_type=F32,
    )
    pair_ref[...] = sums[:DEPTH, :WINDOW]

    @pl.loop(0, 9)
    def _(plane):
        for copies in (halo(plane), pairs(plane)):
            c, u, d = copies

            @pl.when(plane != 4)
            def _():
                c.wait_send()

            u.wait_send()
            d.wait_send()


def body(t_matrix, structure, species, members, delta_table):
    t = t_matrix.reshape(DEPTH, L2, L2).transpose(1, 0, 2).reshape(L2, LANES)
    dtab = jnp.tile(delta_table.reshape(SPECIES, L2, L2), (1, 1, DEPTH))
    vmem = pl.BlockSpec(memory_space=pltpu.VMEM)
    dma = pltpu.SemaphoreType.DMA
    tau, pair = pl.pallas_call(
        kernel,
        out_shape=(
            jax.ShapeDtypeStruct((L2, LANES), F32),
            jax.ShapeDtypeStruct((DEPTH, WINDOW), F32),
        ),
        in_specs=[
            vmem,
            pl.BlockSpec(memory_space=pl.ANY),
            pl.BlockSpec(memory_space=pltpu.SMEM),
            vmem,
            vmem,
        ],
        out_specs=(vmem, vmem),
        scratch_shapes=[
            pltpu.VMEM((ROWS, ROWS), F32),
            pltpu.VMEM((ROWS, PADDED), BF16),
            pltpu.VMEM((ROWS, PADDED), BF16),
            pltpu.VMEM((2, PADDED, 2 * LANES), BF16),
            pltpu.VMEM((WINDOW, 2 * L2, LANES), BF16),
            pltpu.VMEM((9, L2, LANES), F32),
            pltpu.VMEM((9, L2 // 2, LANES), F32),
            pltpu.VMEM((9, L2 // 2, LANES), F32),
            pltpu.VMEM((L2 // 2, LANES), F32),
            pltpu.VMEM((L2 // 2, LANES), F32),
            pltpu.VMEM((48, LANES), F32),
            pltpu.VMEM((LANES, LANES), BF16),
            pltpu.VMEM((2 * LANES, 2 * LANES), BF16),
            pltpu.VMEM((PADDED, LANES), F32),
            pltpu.VMEM((48, L2, LANES), F32),
            pltpu.VMEM((48, LANES), F32),
            pltpu.VMEM((9, 4, L2, LANES), F32),
            pltpu.VMEM((9, L2, LANES), F32),
            pltpu.VMEM((9, L2, LANES), F32),
            pltpu.VMEM((9, 4, L2, LANES), F32),
            pltpu.VMEM((9, L2, LANES), F32),
            pltpu.VMEM((9, L2, LANES), F32),
        ]
        + [dma((9,))] * 13,
        compiler_params=pltpu.CompilerParams(
            collective_id=0, has_side_effects=True, vmem_limit_bytes=56 << 20
        ),
    )(t, structure, species.reshape(DEPTH), members.reshape(DEPTH, WINDOW), dtab)
    tau = tau.reshape(L2, DEPTH, L2).transpose(1, 0, 2)
    return tau.reshape(1, 1, 1, DEPTH, L2 * L2), pair.reshape(1, 1, DEPTH, WINDOW)


def solution(mesh):
    placed = (
        P(None, "gx", "gy", "gz", None),
        P(),
        P("gx", "gy", "gz"),
        P("gx", "gy", "gz", None),
        P(),
    )
    return jax.shard_map(
        body,
        mesh=mesh,
        in_specs=placed,
        out_specs=(P(None, "gx", "gy", "gz", None), P("gx", "gy", "gz", None)),
        check_vma=False,
    )
```

```python
import jax
import jax.numpy as jnp
from jax import lax
from jax.experimental import pallas as pl
from jax.experimental.pallas import tpu as pltpu
from jax.sharding import PartitionSpec as P

L2 = 32
WINDOW = 45
ITERS = 4
SPECIES = 4
DEPTH = 4
LANES = DEPTH * L2
ROWS = WINDOW * L2
PADDED = 1536
CHUNK = ROWS // 3
CELLS = WINDOW // 3
CENTRE = WINDOW // 2
F32 = jnp.float32
BF16 = jnp.bfloat16
MESH = pl.DeviceIdType.MESH


def split(x):
    high = x.astype(BF16)
    return high, (x - high.astype(F32)).astype(BF16)


def dot(a, b):
    return jnp.dot(a, b, preferred_element_type=F32)


def turned4(p):
    q = jnp.concatenate([p, p], axis=0)
    row = lax.broadcasted_iota(jnp.int32, (8, LANES), 0)
    block = lax.broadcasted_iota(jnp.int32, (8, LANES), 1) // L2
    out = q
    for d in range(1, 4):
        moved = pltpu.roll(pltpu.roll(q, L2 * d, 1), 8 - d, 0)
        out = jnp.where((block - row + 8) % 4 == d, moved, out)
    return out[:4]


def kernel(
    t_ref,
    s_hbm,
    species_ref,
    members_ref,
    table_ref,
    tau_ref,
    pair_ref,
    sf,
    sh,
    sl,
    w,
    tw,
    halo_c,
    halo_l,
    halo_r,
    pack_u,
    pack_d,
    mask,
    blocks,
    dbd,
    tc,
    image1,
    rnat,
    rb,
    prow,
    msend,
    usend,
    dsend,
    mrecv,
    urecv,
    drecv,
    s_sem,
    hc_send,
    hl_send,
    hr_send,
    hc_recv,
    hl_recv,
    hr_recv,
    m_send,
    u_send,
    d_send,
    m_recv,
    u_recv,
    d_recv,
):
    gx, gy, gz = lax.axis_index("gx"), lax.axis_index("gy"), lax.axis_index("gz")
    nx, ny, nz = lax.axis_size("gx"), lax.axis_size("gy"), lax.axis_size("gz")

    def peer(dx, dy, dz):
        return (
            lax.rem(gx + dx + nx, nx),
            lax.rem(gy + dy + ny, ny),
            lax.rem(gz + dz + nz, nz),
        )

    def rows_copy(i):
        rows = pl.ds(pl.multiple_of(i * 160, 160), 160)
        return pltpu.make_async_copy(s_hbm.at[0, rows, :], sf.at[rows, :], s_sem.at[i])

    @pl.loop(0, 9)
    def _(i):
        rows_copy(i).start()

    barrier = pltpu.get_barrier_semaphore()

    @pl.loop(0, 27)
    def _(n):
        @pl.when(n != 13)
        def _():
            pl.semaphore_signal(
                barrier,
                inc=1,
                device_id=peer(n // 9 - 1, lax.rem(n // 3, 3) - 1, lax.rem(n, 3) - 1),
                device_id_type=MESH,
            )

    lane = lax.broadcasted_iota(jnp.int32, (L2, LANES), 1)
    lane16 = lax.broadcasted_iota(jnp.int32, (L2 // 2, LANES), 1)
    for k in range(8):
        tc[4 * k : 4 * k + 4, :] = turned4(t_ref[:, k * LANES : (k + 1) * LANES])
    t = tc[...]
    top, low = t[: L2 // 2], t[L2 // 2 :]
    pack_u[...] = jnp.where(lane16 < 64, pltpu.roll(top, 64, 1), low)
    pack_d[...] = jnp.where(lane16 < 64, top, pltpu.roll(low, 64, 1))
    halo_c[4] = t

    pl.semaphore_wait(barrier, 26)

    def remote(src, dst, send, recv, device):
        return pltpu.make_async_remote_copy(
            src_ref=src,
            dst_ref=dst,
            send_sem=send,
            recv_sem=recv,
            device_id=device,
            device_id_type=MESH,
        )

    def halo(plane, aside=True):
        dx, dy = plane // 3 - 1, lax.rem(plane, 3) - 1
        slot = 8 - plane
        c = None
        if aside:
            c = remote(tc, halo_c.at[slot], hc_send.at[plane], hc_recv.at[slot], peer(dx, dy, 0))
        u = remote(pack_u, halo_l.at[slot], hl_send.at[plane], hl_recv.at[slot], peer(dx, dy, 1))
        d = remote(pack_d, halo_r.at[slot], hr_send.at[plane], hr_recv.at[slot], peer(dx, dy, -1))
        return c, u, d

    @pl.loop(0, 9)
    def _(plane):
        c, u, d = halo(plane)

        @pl.when(plane != 4)
        def _():
            c.start()

        u.start()
        d.start()

    cells = lax.broadcasted_iota(jnp.int32, (48, WINDOW), 0)
    lane48 = lax.broadcasted_iota(jnp.int32, (48, LANES), 1)
    member = jnp.zeros((48, LANES), F32)
    for s in range(DEPTH):
        hit = jnp.where(members_ref[s : s + 1, :] == cells, 1.0, 0.0).astype(F32)
        some = jnp.max(hit, axis=1, keepdims=True)
        member = jnp.where(lane48 // L2 == s, some, member)
    mask[...] = member

    br = lax.broadcasted_iota(jnp.int32, (LANES, LANES), 0)
    bc = lax.broadcasted_iota(jnp.int32, (LANES, LANES), 1)
    blocks[...] = jnp.where(br // L2 == bc // L2, 1.0, 0.0).astype(BF16)

    deltas = jnp.concatenate(
        [turned4(table_ref[:, k * LANES : (k + 1) * LANES]) for k in range(8)], axis=0
    )
    code = jnp.zeros((L2, LANES), jnp.int32)
    for s in range(DEPTH):
        code = jnp.where(lane // L2 == s, s + 4 - species_ref[s], code)
    code = code % 4
    chosen = deltas
    for m in range(1, 4):
        chosen = jnp.where(code == m, pltpu.roll(deltas, L2 * m, 1), chosen)
    for s in range(DEPTH):
        dh, dl = split(jnp.where(lane // L2 == s, chosen, 0.0))
        rows = slice(s * L2, (s + 1) * L2)
        down = slice(LANES + s * L2, LANES + (s + 1) * L2)
        dbd[rows, :LANES] = dh
        dbd[rows, LANES:] = dl
        dbd[down, :LANES] = dh
        dbd[down, LANES:] = jnp.zeros((L2, LANES), BF16)

    w[:, 512:768, :] = jnp.zeros((2, 256, 2 * LANES), BF16)
    w[:, ROWS:, :] = jnp.zeros((2, PADDED - ROWS, 2 * LANES), BF16)
    th, tl = split(t)
    w[0, CENTRE * L2 : (CENTRE + 1) * L2, :LANES] = th
    w[0, CENTRE * L2 : (CENTRE + 1) * L2, LANES:] = tl
    sh[:, ROWS:] = jnp.zeros((ROWS, PADDED - ROWS), BF16)
    sl[:, ROWS:] = jnp.zeros((ROWS, PADDED - ROWS), BF16)

    @pl.loop(0, 3)
    def _(i):
        for j in range(3):
            rows_copy(3 * i + j).wait()
        rows = pl.ds(pl.multiple_of(i * CHUNK, CHUNK), CHUNK)
        high, rest = split(sf[rows, :])
        sh[rows, :ROWS] = high
        sl[rows, :ROWS] = rest

    wide = w[0, 512:768, :]
    a = dot(sh[:, 512:768], wide)
    b = dot(sl[:, 512:768], wide[:, :LANES])
    image1[...] = a[:, :LANES] + (a[:, LANES:] + b)

    def windows_of(plane):
        c, u, d = halo(8 - plane, plane != 4)
        if plane != 4:
            c.wait_recv()
        u.wait_recv()
        d.wait_recv()
        centre = halo_c[plane]
        up, down = halo_l[plane], halo_r[plane]
        left = jnp.concatenate([pltpu.roll(up, 64, 1), up], axis=0)
        right = jnp.concatenate([down, pltpu.roll(down, 64, 1)], axis=0)
        windows = [
            pltpu.roll(jnp.where(lane < 64, centre, left), 64, 1),
            pltpu.roll(jnp.where(lane < 96, centre, left), 32, 1),
            centre,
            pltpu.roll(jnp.where(lane < 32, right, centre), 96, 1),
            pltpu.roll(jnp.where(lane < 64, right, centre), 64, 1),
        ]
        for k in range(5):
            cell = plane * 5 + k
            th, tl = split(windows[k] * mask[cell : cell + 1, :])
            tw[cell, :L2] = th
            tw[cell, L2:] = tl

    def blocks_times(image, cell, on):
        ih, il = split(image)
        wbd = jnp.concatenate(
            [
                jnp.concatenate([ih] * DEPTH, axis=0) * on,
                jnp.concatenate([il] * DEPTH, axis=0) * on,
            ],
            axis=1,
        )
        res = dot(tw[cell], wbd)
        x = res[:L2, :LANES] + (res[:L2, LANES:] + res[L2:, :LANES])
        return x + tc[...] if cell == CENTRE else x

    def both(x):
        return jnp.concatenate(split(x), axis=1)

    def images(rows, now):
        wide = w[now]
        a = dot(sh[rows, :], wide)
        b = dot(sl[rows, :], wide[:, :LANES])
        return a[:, :LANES] + (a[:, LANES:] + b)

    def sweep(now, later):
        image = images(slice(0, ROWS), now)
        on = blocks[...]
        for cell in range(WINDOW):
            rows = slice(cell * L2, (cell + 1) * L2)
            w[later, rows, :] = both(blocks_times(image[rows], cell, on))

    def last_sweep(now, g):
        start = g * CHUNK
        image = images(slice(start, start + CHUNK), now)
        on = blocks[...]
        columns = []
        for i in range(CELLS):
            cell = g * CELLS + i
            x = blocks_times(image[i * L2 : (i + 1) * L2], cell, on)
            if cell == CENTRE:
                for k in range(8):
                    tau_ref[:, k * LANES : (k + 1) * LANES] = turned4(x[4 * k : 4 * k + 4])
            columns.append(both(x))
        r2 = dot(jnp.concatenate(columns, axis=0), dbd[...])
        r = r2[:, :LANES] + r2[:, LANES:]
        rnat[start : start + CHUNK, :] = r
        for j in range(3):
            turned = []
            for k in range(5):
                at = (j * 5 + k) * L2
                block = r[at : at + L2]
                turned.append(pltpu.roll(block, (L2 * (k - 2)) % LANES, 1) if k != 2 else block)
            plane = g * 3 + j
            target = mrecv if plane == 4 else msend
            usend[plane] = jnp.where(lane < 64, turned[4], pltpu.roll(turned[3], 64, 1))
            dsend[plane] = jnp.where(lane >= 64, turned[0], pltpu.roll(turned[1], 64, 1))
            target[plane, 0] = turned[2]
            target[plane, 1] = turned[3]
            target[plane, 2] = turned[1]
            target[plane, 3] = jnp.where(lane >= 64, turned[4], turned[0])
            c, u, d = pairs(plane, plane != 4)
            if plane != 4:
                c.start()
            u.start()
            d.start()

    def pairs(plane, aside=True):
        dx, dy = plane // 3 - 1, lax.rem(plane, 3) - 1
        c = None
        if aside:
            c = remote(msend.at[plane], mrecv.at[plane], m_send.at[plane], m_recv.at[plane], peer(dx, dy, 0))
        u = remote(usend.at[plane], urecv.at[plane], u_send.at[plane], u_recv.at[plane], peer(dx, dy, 1))
        d = remote(dsend.at[plane], drecv.at[plane], d_send.at[plane], d_recv.at[plane], peer(dx, dy, -1))
        return c, u, d

    for g in (1, 0, 2):
        for j in range(3):
            windows_of(3 * g + j)
        on = blocks[...]
        for cell in range(g * CELLS, (g + 1) * CELLS):
            rows = slice(cell * L2, (cell + 1) * L2)
            w[1, rows, :] = both(blocks_times(image1[rows, :], cell, on))

    @pl.loop(1, ITERS - 1)
    def _(n):
        now = lax.rem(n, 2)
        sweep(now, 1 - now)

    for g in (0, 2, 1):
        last_sweep((ITERS - 1) % 2, g)

    rnat[ROWS:, :] = jnp.zeros((PADDED - ROWS, LANES), F32)

    @pl.loop(0, 3)
    def _(n):
        for m in range(4):
            i = 4 * n + m
            turned = rnat[pl.ds(pl.multiple_of(i * LANES, LANES), LANES), :].T
            for j in range(4):
                out = None
                for s in range(DEPTH):
                    part = turned[s * L2 : (s + 1) * L2]
                    shift = (L2 * (s - j)) % LANES
                    part = pltpu.roll(part, shift, 1) if shift else part
                    out = part if out is None else jnp.where(lane // L2 == s, part, out)
                rb[i * 4 + j] = out

    @pl.loop(0, 9)
    def _(n):
        plane = jnp.where(n == 0, 4, jnp.where(n <= 4, n - 1, n))
        c, u, d = pairs(plane)

        @pl.when(n != 0)
        def _():
            c.wait_recv()

        u.wait_recv()
        d.wait_recv()
        up, down = urecv[plane], drecv[plane]
        split_block = mrecv[plane, 3]
        got = [
            jnp.where(lane < 64, split_block, down),
            jnp.where(lane < 96, mrecv[plane, 2], pltpu.roll(down, 64, 1)),
            mrecv[plane, 0],
            jnp.where(lane < 32, pltpu.roll(up, 64, 1), mrecv[plane, 1]),
            jnp.where(lane < 64, up, split_block),
        ]
        for k in range(5):
            cell = WINDOW - 1 - (plane * 5 + k)
            prow[pl.ds(cell, 1), :] = jnp.sum(got[k] * rb[cell], axis=0, keepdims=True)

    prow[WINDOW:, :] = jnp.zeros((48 - WINDOW, LANES), F32)
    sr = lax.broadcasted_iota(jnp.int32, (8, LANES), 0)
    sc = lax.broadcasted_iota(jnp.int32, (8, LANES), 1)
    summed = jnp.where(sc // L2 == sr, 1.0, 0.0).astype(F32)
    sums = lax.dot_general(
        summed,
        prow[...],
        (((1,), (1,)), ((), ())),
        precision=lax.Precision.HIGHEST,
        preferred_element_type=F32,
    )
    pair_ref[...] = sums[:DEPTH, :WINDOW]

    @pl.loop(0, 9)
    def _(plane):
        for copies in (halo(plane), pairs(plane)):
            c, u, d = copies

            @pl.when(plane != 4)
            def _():
                c.wait_send()

            u.wait_send()
            d.wait_send()


def body(t_matrix, structure, species, members, delta_table):
    vmem = pl.BlockSpec(memory_space=pltpu.VMEM)
    dma = pltpu.SemaphoreType.DMA
    tau, pair = pl.pallas_call(
        kernel,
        out_shape=(
            jax.ShapeDtypeStruct((DEPTH, L2 * L2), F32),
            jax.ShapeDtypeStruct((DEPTH, WINDOW), F32),
        ),
        in_specs=[
            vmem,
            pl.BlockSpec(memory_space=pltpu.HBM),
            pl.BlockSpec(memory_space=pltpu.SMEM),
            vmem,
            vmem,
        ],
        out_specs=(vmem, vmem),
        scratch_shapes=[
            pltpu.VMEM((ROWS, ROWS), F32),
            pltpu.VMEM((ROWS, PADDED), BF16),
            pltpu.VMEM((ROWS, PADDED), BF16),
            pltpu.VMEM((2, PADDED, 2 * LANES), BF16),
            pltpu.VMEM((WINDOW, 2 * L2, LANES), BF16),
            pltpu.VMEM((9, L2, LANES), F32),
            pltpu.VMEM((9, L2 // 2, LANES), F32),
            pltpu.VMEM((9, L2 // 2, LANES), F32),
            pltpu.VMEM((L2 // 2, LANES), F32),
            pltpu.VMEM((L2 // 2, LANES), F32),
            pltpu.VMEM((48, LANES), F32),
            pltpu.VMEM((LANES, LANES), BF16),
            pltpu.VMEM((2 * LANES, 2 * LANES), BF16),
            pltpu.VMEM((L2, LANES), F32),
            pltpu.VMEM((ROWS, LANES), F32),
            pltpu.VMEM((PADDED, LANES), F32),
            pltpu.VMEM((48, L2, LANES), F32),
            pltpu.VMEM((48, LANES), F32),
            pltpu.VMEM((9, 4, L2, LANES), F32),
            pltpu.VMEM((9, L2, LANES), F32),
            pltpu.VMEM((9, L2, LANES), F32),
            pltpu.VMEM((9, 4, L2, LANES), F32),
            pltpu.VMEM((9, L2, LANES), F32),
            pltpu.VMEM((9, L2, LANES), F32),
        ]
        + [dma((9,))] * 13,
        compiler_params=pltpu.CompilerParams(
            collective_id=0, has_side_effects=True, vmem_limit_bytes=57 << 20
        ),
    )(
        t_matrix.reshape(DEPTH, L2 * L2),
        structure,
        species.reshape(DEPTH),
        members.reshape(DEPTH, WINDOW),
        delta_table,
    )
    return tau.reshape(1, 1, 1, DEPTH, L2 * L2), pair.reshape(1, 1, DEPTH, WINDOW)


def solution(mesh):
    placed = (
        P(None, "gx", "gy", "gz", None),
        P(),
        P("gx", "gy", "gz"),
        P("gx", "gy", "gz", None),
        P(),
    )
    return jax.shard_map(
        body,
        mesh=mesh,
        in_specs=placed,
        out_specs=(P(None, "gx", "gy", "gz", None), P("gx", "gy", "gz", None)),
        check_vma=False,
    )
```

```python
import jax
import jax.numpy as jnp
from jax import lax
from jax.experimental import pallas as pl
from jax.experimental.pallas import tpu as pltpu
from jax.sharding import PartitionSpec as P

L2 = 32
WINDOW = 45
ITERS = 4
SPECIES = 4
DEPTH = 4
LANES = DEPTH * L2
ROWS = WINDOW * L2
PADDED = 1536
CHUNK = ROWS // 3
CELLS = WINDOW // 3
CENTRE = WINDOW // 2
F32 = jnp.float32
BF16 = jnp.bfloat16
MESH = pl.DeviceIdType.MESH
ORDER = (0, 8, 2, 6, 3, 5, 1, 7, 4)
OFFSETS = sorted(
    [(x, y, z) for x in (-1, 0, 1) for y in (-1, 0, 1) for z in (-1, 0, 1) if x or y or z],
    key=lambda o: -(abs(o[0]) + abs(o[1]) + abs(o[2])),
)


def cell_at(position):
    return ORDER[position // 5] * 5 + position % 5


def split(x):
    high = x.astype(BF16)
    return high, (x - high.astype(F32)).astype(BF16)


def dot(a, b):
    return jnp.dot(a, b, preferred_element_type=F32)


def turned4(p):
    q = jnp.concatenate([p, p], axis=0)
    row = lax.broadcasted_iota(jnp.int32, (8, LANES), 0)
    block = lax.broadcasted_iota(jnp.int32, (8, LANES), 1) // L2
    out = q
    for d in range(1, 4):
        moved = pltpu.roll(pltpu.roll(q, L2 * d, 1), 8 - d, 0)
        out = jnp.where((block - row + 8) % 4 == d, moved, out)
    return out[:4]


def kernel(
    t_ref,
    s_hbm,
    species_ref,
    members_ref,
    table_ref,
    tau_ref,
    pair_ref,
    sf,
    sh,
    sl,
    w,
    tw,
    halo_c,
    halo_l,
    halo_r,
    pack_u,
    pack_d,
    mask,
    blocks,
    dbd,
    tc,
    image1,
    rnat,
    rb,
    prow,
    msend,
    usend,
    dsend,
    mrecv,
    urecv,
    drecv,
    s_sem,
    hc_send,
    hl_send,
    hr_send,
    hc_recv,
    hl_recv,
    hr_recv,
    m_send,
    u_send,
    d_send,
    m_recv,
    u_recv,
    d_recv,
):
    gx, gy, gz = lax.axis_index("gx"), lax.axis_index("gy"), lax.axis_index("gz")
    nx, ny, nz = lax.axis_size("gx"), lax.axis_size("gy"), lax.axis_size("gz")

    xs = (lax.rem(gx + nx - 1, nx), gx, lax.rem(gx + 1, nx))
    ys = (lax.rem(gy + ny - 1, ny), gy, lax.rem(gy + 1, ny))
    zs = (lax.rem(gz + nz - 1, nz), gz, lax.rem(gz + 1, nz))

    def peer(dx, dy, dz):
        return (xs[dx + 1], ys[dy + 1], zs[dz + 1])

    barrier = pltpu.get_barrier_semaphore()
    for offset in OFFSETS:
        pl.semaphore_signal(barrier, inc=1, device_id=peer(*offset), device_id_type=MESH)

    def rows_copy(i):
        return pltpu.make_async_copy(
            s_hbm.at[0, pl.ds(ORDER[i] * 160, 160), :],
            sf.at[pl.ds(i * 160, 160), :],
            s_sem.at[i],
        )

    for i in range(9):
        rows_copy(i).start()

    lane = lax.broadcasted_iota(jnp.int32, (L2, LANES), 1)
    lane8 = lax.broadcasted_iota(jnp.int32, (8, LANES), 1)
    lane16 = lax.broadcasted_iota(jnp.int32, (L2 // 2, LANES), 1)
    for k in range(8):
        tc[4 * k : 4 * k + 4, :] = turned4(t_ref[:, k * LANES : (k + 1) * LANES])
    t = tc[...]
    top, low = t[: L2 // 2], t[L2 // 2 :]
    pack_u[...] = jnp.where(lane16 < 64, pltpu.roll(top, 64, 1), low)
    pack_d[...] = jnp.where(lane16 < 64, top, pltpu.roll(low, 64, 1))
    halo_c[4] = t

    pl.semaphore_wait(barrier, 26)

    def remote(src, dst, send, recv, device):
        return pltpu.make_async_remote_copy(
            src_ref=src,
            dst_ref=dst,
            send_sem=send,
            recv_sem=recv,
            device_id=device,
            device_id_type=MESH,
        )

    def halo(offset):
        dx, dy, dz = offset
        plane = (dx + 1) * 3 + dy + 1
        slot = 8 - plane
        source = (pack_d, tc, pack_u)[dz + 1]
        target = (halo_r, halo_c, halo_l)[dz + 1]
        send = (hr_send, hc_send, hl_send)[dz + 1]
        recv = (hr_recv, hc_recv, hl_recv)[dz + 1]
        return remote(source, target.at[slot], send.at[plane], recv.at[slot], peer(*offset))

    for offset in OFFSETS:
        halo(offset).start()

    cells = lax.broadcasted_iota(jnp.int32, (48, WINDOW), 0)
    lane48 = lax.broadcasted_iota(jnp.int32, (48, LANES), 1)
    member = jnp.zeros((48, LANES), F32)
    for s in range(DEPTH):
        hit = jnp.where(members_ref[s : s + 1, :] == cells, 1.0, 0.0).astype(F32)
        some = jnp.max(hit, axis=1, keepdims=True)
        member = jnp.where(lane48 // L2 == s, some, member)
    mask[...] = member

    br = lax.broadcasted_iota(jnp.int32, (LANES, LANES), 0)
    bc = lax.broadcasted_iota(jnp.int32, (LANES, LANES), 1)
    blocks[...] = jnp.where(br // L2 == bc // L2, 1.0, 0.0).astype(BF16)

    deltas = jnp.concatenate(
        [turned4(table_ref[:, k * LANES : (k + 1) * LANES]) for k in range(8)], axis=0
    )
    code = jnp.zeros((L2, LANES), jnp.int32)
    for s in range(DEPTH):
        code = jnp.where(lane // L2 == s, s + 4 - species_ref[s], code)
    code = code % 4
    chosen = deltas
    for m in range(1, 4):
        chosen = jnp.where(code == m, pltpu.roll(deltas, L2 * m, 1), chosen)
    for s in range(DEPTH):
        dh, dl = split(jnp.where(lane // L2 == s, chosen, 0.0))
        rows = slice(s * L2, (s + 1) * L2)
        down = slice(LANES + s * L2, LANES + (s + 1) * L2)
        dbd[rows, :LANES] = dh
        dbd[rows, LANES:] = dl
        dbd[down, :LANES] = dh
        dbd[down, LANES:] = jnp.zeros((L2, LANES), BF16)

    w[:, 512:768, :] = jnp.zeros((2, 256, 2 * LANES), BF16)
    w[:, ROWS:, :] = jnp.zeros((2, PADDED - ROWS, 2 * LANES), BF16)
    th, tl = split(t)
    w[0, CENTRE * L2 : (CENTRE + 1) * L2, :LANES] = th
    w[0, CENTRE * L2 : (CENTRE + 1) * L2, LANES:] = tl
    sh[:, ROWS:] = jnp.zeros((ROWS, PADDED - ROWS), BF16)
    sl[:, ROWS:] = jnp.zeros((ROWS, PADDED - ROWS), BF16)

    for i in range(3):
        for j in range(3):
            rows_copy(3 * i + j).wait()
        rows = pl.ds(i * CHUNK, CHUNK)
        high, rest = split(sf[rows, :])
        sh[rows, :ROWS] = high
        sl[rows, :ROWS] = rest

    wide = w[0, 512:768, :]
    a = dot(sh[:, 512:768], wide)
    b = dot(sl[:, 512:768], wide[:, :LANES])
    image1[...] = a[:, :LANES] + (a[:, LANES:] + b)

    def windows_of(plane):
        dx, dy = plane // 3 - 1, plane % 3 - 1
        for dz in (-1, 0, 1):
            if (dx, dy, dz) != (0, 0, 0):
                halo((-dx, -dy, -dz)).wait_recv()
        centre = halo_c[plane]
        up, down = halo_l[plane], halo_r[plane]
        left = jnp.concatenate([pltpu.roll(up, 64, 1), up], axis=0)
        right = jnp.concatenate([down, pltpu.roll(down, 64, 1)], axis=0)
        windows = [
            pltpu.roll(jnp.where(lane < 64, centre, left), 64, 1),
            pltpu.roll(jnp.where(lane < 96, centre, left), 32, 1),
            centre,
            pltpu.roll(jnp.where(lane < 32, right, centre), 96, 1),
            pltpu.roll(jnp.where(lane < 64, right, centre), 64, 1),
        ]
        for k in range(5):
            cell = plane * 5 + k
            th, tl = split(windows[k] * mask[cell : cell + 1, :])
            tw[cell, :L2] = th
            tw[cell, L2:] = tl

    def blocks_times(image, cell, on):
        ih, il = split(image)
        wbd = jnp.concatenate(
            [
                jnp.concatenate([ih] * DEPTH, axis=0) * on,
                jnp.concatenate([il] * DEPTH, axis=0) * on,
            ],
            axis=1,
        )
        res = dot(tw[cell], wbd)
        x = res[:L2, :LANES] + (res[:L2, LANES:] + res[L2:, :LANES])
        return x + tc[...] if cell == CENTRE else x

    def both(x):
        return jnp.concatenate(split(x), axis=1)

    def images(rows, now):
        wide = w[now]
        a = dot(sh[rows, :], wide)
        b = dot(sl[rows, :], wide[:, :LANES])
        return a[:, :LANES] + (a[:, LANES:] + b)

    def sweep(now, later):
        image = images(slice(0, ROWS), now)
        on = blocks[...]
        for i in range(WINDOW):
            cell = cell_at(i)
            x = blocks_times(image[i * L2 : (i + 1) * L2], cell, on)
            w[later, cell * L2 : (cell + 1) * L2, :] = both(x)

    def last_sweep(now, planes):
        start = planes[0] * 160
        size = len(planes) * 160
        image = images(slice(start, start + size), now)
        on = blocks[...]
        columns = []
        for i in range(size // L2):
            cell = cell_at(planes[0] * 5 + i)
            x = blocks_times(image[i * L2 : (i + 1) * L2], cell, on)
            if cell == CENTRE:
                for k in range(8):
                    tau_ref[:, k * LANES : (k + 1) * LANES] = turned4(x[4 * k : 4 * k + 4])
            columns.append(both(x))
        r2 = dot(jnp.concatenate(columns, axis=0), dbd[...])
        r = r2[:, :LANES] + r2[:, LANES:]
        for j, position in enumerate(planes):
            plane = ORDER[position]
            rnat[plane * 160 : (plane + 1) * 160, :] = r[j * 160 : (j + 1) * 160]
            turned = []
            for k in range(5):
                at = j * 160 + k * L2
                block = r[at : at + L2]
                turned.append(pltpu.roll(block, (L2 * (k - 2)) % LANES, 1) if k != 2 else block)
            usend[plane, :16] = jnp.where(
                lane16 < 64, turned[4][:16], pltpu.roll(turned[4][16:], 64, 1)
            )
            usend[plane, 16:] = quarter(turned[3], 0)
            dsend[plane, :16] = jnp.where(
                lane16 >= 64, turned[0][:16], pltpu.roll(turned[0][16:], 64, 1)
            )
            dsend[plane, 16:] = quarter(turned[1], 3)
            target = mrecv if plane == 4 else msend
            target[plane, :32] = turned[2]
            target[plane, 32:64] = jnp.where(lane >= 64, turned[4], turned[0])
            target[plane, 64:96] = jnp.where(lane < 32, turned[1], turned[3])
            target[plane, 96:] = jnp.where(
                (lane16 >= 32) & (lane16 < 96), turned[1][:16], pltpu.roll(turned[1][16:], 64, 1)
            )
            for dz in (-1, 1, 0):
                if plane != 4 or dz:
                    pairs(plane, dz).start()

    def quarter(x, first):
        out = x[:8]
        for m in range(1, 4):
            moved = pltpu.roll(x[8 * m : 8 * m + 8], L2 * m, 1)
            out = jnp.where(lane8 // L2 == (first + m) % 4, moved, out)
        return out

    def unquarter(q):
        parts = [q] + [pltpu.roll(q, LANES - L2 * m, 1) for m in range(1, 4)]
        return jnp.concatenate(parts, axis=0)

    def unhalf(h):
        return jnp.concatenate([h, pltpu.roll(h, 64, 1)], axis=0)

    def pairs(plane, dz):
        dx, dy = plane // 3 - 1, plane % 3 - 1
        source = (dsend, msend, usend)[dz + 1]
        target = (drecv, mrecv, urecv)[dz + 1]
        send = (d_send, m_send, u_send)[dz + 1]
        recv = (d_recv, m_recv, u_recv)[dz + 1]
        return remote(
            source.at[plane], target.at[plane], send.at[plane], recv.at[plane], peer(dx, dy, dz)
        )

    for first, past in ((4, 9), (0, 4)):
        for position in range(past - 1, first - 1, -1):
            windows_of(ORDER[position])
        on = blocks[...]
        for i in range(first * 5, past * 5):
            cell = cell_at(i)
            x = blocks_times(image1[i * L2 : (i + 1) * L2, :], cell, on)
            w[1, cell * L2 : (cell + 1) * L2, :] = both(x)

    @pl.loop(1, ITERS - 1)
    def _(n):
        now = lax.rem(n, 2)
        sweep(now, 1 - now)

    for planes in ((0, 1), (2, 3), (4, 5), (6, 7), (8,)):
        last_sweep((ITERS - 1) % 2, planes)

    rnat[ROWS:, :] = jnp.zeros((PADDED - ROWS, LANES), F32)

    @pl.loop(0, 3)
    def _(n):
        for m in range(4):
            i = 4 * n + m
            turned = rnat[pl.ds(pl.multiple_of(i * LANES, LANES), LANES), :].T
            for j in range(4):
                out = None
                for s in range(DEPTH):
                    part = turned[s * L2 : (s + 1) * L2]
                    shift = (L2 * (s - j)) % LANES
                    part = pltpu.roll(part, shift, 1) if shift else part
                    out = part if out is None else jnp.where(lane // L2 == s, part, out)
                rb[i * 4 + j] = out

    for plane in ORDER:
        for dz in (-1, 0, 1):
            if plane != 4 or dz:
                pairs(plane, dz).wait_recv()
        u2, u1 = unhalf(urecv[plane, :16]), unquarter(urecv[plane, 16:])
        d2, d1 = unhalf(drecv[plane, :16]), unquarter(drecv[plane, 16:])
        outer, inner = mrecv[plane, 32:64], mrecv[plane, 64:96]
        rest = unhalf(mrecv[plane, 96:])
        got = [
            jnp.where(lane < 64, outer, d2),
            jnp.where(lane < 32, inner, jnp.where(lane < 96, rest, d1)),
            mrecv[plane, :32],
            jnp.where(lane < 32, u1, inner),
            jnp.where(lane < 64, u2, outer),
        ]
        for k in range(5):
            cell = WINDOW - 1 - (plane * 5 + k)
            prow[cell : cell + 1, :] = jnp.sum(got[k] * rb[cell], axis=0, keepdims=True)

    prow[WINDOW:, :] = jnp.zeros((48 - WINDOW, LANES), F32)
    sr = lax.broadcasted_iota(jnp.int32, (8, LANES), 0)
    sc = lax.broadcasted_iota(jnp.int32, (8, LANES), 1)
    summed = jnp.where(sc // L2 == sr, 1.0, 0.0).astype(F32)
    sums = lax.dot_general(
        summed,
        prow[...],
        (((1,), (1,)), ((), ())),
        precision=lax.Precision.HIGHEST,
        preferred_element_type=F32,
    )
    pair_ref[...] = sums[:DEPTH, :WINDOW]

    for offset in OFFSETS:
        halo(offset).wait_send()
    for plane in ORDER:
        for dz in (-1, 0, 1):
            if plane != 4 or dz:
                pairs(plane, dz).wait_send()


def finish(tau_ref, pair_ref, tau_out, pair_out, sem):
    copies = (
        pltpu.make_async_copy(tau_ref, tau_out, sem.at[0]),
        pltpu.make_async_copy(pair_ref, pair_out, sem.at[1]),
    )
    for copy in copies:
        copy.start()
    for copy in copies:
        copy.wait()


def body(t_matrix, structure, species, members, delta_table):
    vmem = pl.BlockSpec(memory_space=pltpu.VMEM)
    dma = pltpu.SemaphoreType.DMA
    tau, pair = pl.pallas_call(
        kernel,
        out_shape=(
            jax.ShapeDtypeStruct((DEPTH, L2 * L2), F32),
            jax.ShapeDtypeStruct((DEPTH, WINDOW), F32),
        ),
        in_specs=[
            vmem,
            pl.BlockSpec(memory_space=pltpu.HBM),
            pl.BlockSpec(memory_space=pltpu.SMEM),
            vmem,
            vmem,
        ],
        out_specs=(vmem, vmem),
        scratch_shapes=[
            pltpu.VMEM((ROWS, ROWS), F32),
            pltpu.VMEM((ROWS, PADDED), BF16),
            pltpu.VMEM((ROWS, PADDED), BF16),
            pltpu.VMEM((2, PADDED, 2 * LANES), BF16),
            pltpu.VMEM((WINDOW, 2 * L2, LANES), BF16),
            pltpu.VMEM((9, L2, LANES), F32),
            pltpu.VMEM((9, L2 // 2, LANES), F32),
            pltpu.VMEM((9, L2 // 2, LANES), F32),
            pltpu.VMEM((L2 // 2, LANES), F32),
            pltpu.VMEM((L2 // 2, LANES), F32),
            pltpu.VMEM((48, LANES), F32),
            pltpu.VMEM((LANES, LANES), BF16),
            pltpu.VMEM((2 * LANES, 2 * LANES), BF16),
            pltpu.VMEM((L2, LANES), F32),
            pltpu.VMEM((ROWS, LANES), F32),
            pltpu.VMEM((PADDED, LANES), F32),
            pltpu.VMEM((48, L2, LANES), F32),
            pltpu.VMEM((48, LANES), F32),
            pltpu.VMEM((9, 112, LANES), F32),
            pltpu.VMEM((9, 24, LANES), F32),
            pltpu.VMEM((9, 24, LANES), F32),
            pltpu.VMEM((9, 112, LANES), F32),
            pltpu.VMEM((9, 24, LANES), F32),
            pltpu.VMEM((9, 24, LANES), F32),
        ]
        + [dma((9,))] * 13,
        compiler_params=pltpu.CompilerParams(
            collective_id=0, has_side_effects=True, vmem_limit_bytes=57 << 20
        ),
    )(
        t_matrix.reshape(DEPTH, L2 * L2),
        structure,
        species.reshape(DEPTH),
        members.reshape(DEPTH, WINDOW),
        delta_table,
    )
    anywhere = pl.BlockSpec(memory_space=pl.ANY)
    tau, pair = pl.pallas_call(
        finish,
        out_shape=(
            jax.ShapeDtypeStruct((DEPTH, L2 * L2), F32),
            jax.ShapeDtypeStruct((DEPTH, WINDOW), F32),
        ),
        in_specs=[anywhere] * 2,
        out_specs=(anywhere,) * 2,
        scratch_shapes=[dma((2,))],
        compiler_params=pltpu.CompilerParams(vmem_limit_bytes=60 << 20),
    )(tau, pair)
    return tau.reshape(1, 1, 1, DEPTH, L2 * L2), pair.reshape(1, 1, DEPTH, WINDOW)


def solution(mesh):
    placed = (
        P(None, "gx", "gy", "gz", None),
        P(),
        P("gx", "gy", "gz"),
        P("gx", "gy", "gz", None),
        P(),
    )
    return jax.shard_map(
        body,
        mesh=mesh,
        in_specs=placed,
        out_specs=(P(None, "gx", "gy", "gz", None), P("gx", "gy", "gz", None)),
        check_vma=False,
    )
```

```python
import jax
import jax.numpy as jnp
from jax import lax
from jax.experimental import pallas as pl
from jax.experimental.pallas import tpu as pltpu
from jax.sharding import PartitionSpec as P

L2 = 32
WINDOW = 45
ITERS = 4
SPECIES = 4
DEPTH = 4
LANES = DEPTH * L2
ROWS = WINDOW * L2
PADDED = 1536
CHUNK = ROWS // 3
CELLS = WINDOW // 3
CENTRE = WINDOW // 2
F32 = jnp.float32
BF16 = jnp.bfloat16
MESH = pl.DeviceIdType.MESH
ORDER = (0, 8, 2, 6, 3, 5, 1, 7, 4)
OFFSETS = sorted(
    [(x, y, z) for x in (-1, 0, 1) for y in (-1, 0, 1) for z in (-1, 0, 1) if x or y or z],
    key=lambda o: -(abs(o[0]) + abs(o[1]) + abs(o[2])),
)


def cell_at(position):
    return ORDER[position // 5] * 5 + position % 5


def split(x):
    high = x.astype(BF16)
    return high, (x - high.astype(F32)).astype(BF16)


def dot(a, b):
    return jnp.dot(a, b, preferred_element_type=F32)


def turned4(p):
    q = jnp.concatenate([p, p], axis=0)
    row = lax.broadcasted_iota(jnp.int32, (8, LANES), 0)
    block = lax.broadcasted_iota(jnp.int32, (8, LANES), 1) // L2
    out = q
    for d in range(1, 4):
        moved = pltpu.roll(pltpu.roll(q, L2 * d, 1), 8 - d, 0)
        out = jnp.where((block - row + 8) % 4 == d, moved, out)
    return out[:4]


def kernel(
    t_hbm,
    s_hbm,
    species_hbm,
    members_hbm,
    table_hbm,
    tau_ref,
    pair_ref,
    t_ref,
    species_ref,
    members_ref,
    table_ref,
    sf,
    sh,
    sl,
    w,
    tw,
    halo_c,
    halo_l,
    halo_r,
    pack_u,
    pack_d,
    mask,
    blocks,
    dbd,
    tc,
    image1,
    rnat,
    rb,
    prow,
    msend,
    usend,
    dsend,
    mrecv,
    urecv,
    drecv,
    in_sem,
    s_sem,
    hc_send,
    hl_send,
    hr_send,
    hc_recv,
    hl_recv,
    hr_recv,
    m_send,
    u_send,
    d_send,
    m_recv,
    u_recv,
    d_recv,
):
    gx, gy, gz = lax.axis_index("gx"), lax.axis_index("gy"), lax.axis_index("gz")
    nx, ny, nz = lax.axis_size("gx"), lax.axis_size("gy"), lax.axis_size("gz")

    xs = (lax.rem(gx + nx - 1, nx), gx, lax.rem(gx + 1, nx))
    ys = (lax.rem(gy + ny - 1, ny), gy, lax.rem(gy + 1, ny))
    zs = (lax.rem(gz + nz - 1, nz), gz, lax.rem(gz + 1, nz))

    def peer(dx, dy, dz):
        return (xs[dx + 1], ys[dy + 1], zs[dz + 1])

    inputs = [
        pltpu.make_async_copy(source, target, in_sem.at[i])
        for i, (source, target) in enumerate(
            (
                (t_hbm, t_ref),
                (species_hbm, species_ref),
                (members_hbm, members_ref),
                (table_hbm, table_ref),
            )
        )
    ]
    for copy in inputs:
        copy.start()

    barrier = pltpu.get_barrier_semaphore()
    for offset in OFFSETS:
        pl.semaphore_signal(barrier, inc=1, device_id=peer(*offset), device_id_type=MESH)

    def rows_copy(i):
        return pltpu.make_async_copy(
            s_hbm.at[0, pl.ds(ORDER[i] * 160, 160), :],
            sf.at[pl.ds(i * 160, 160), :],
            s_sem.at[i],
        )

    for i in range(9):
        rows_copy(i).start()

    lane = lax.broadcasted_iota(jnp.int32, (L2, LANES), 1)
    lane8 = lax.broadcasted_iota(jnp.int32, (8, LANES), 1)
    lane16 = lax.broadcasted_iota(jnp.int32, (L2 // 2, LANES), 1)
    inputs[0].wait()
    for k in range(8):
        tc[4 * k : 4 * k + 4, :] = turned4(t_ref[:, k * LANES : (k + 1) * LANES])
    t = tc[...]
    top, low = t[: L2 // 2], t[L2 // 2 :]
    pack_u[...] = jnp.where(lane16 < 64, pltpu.roll(top, 64, 1), low)
    pack_d[...] = jnp.where(lane16 < 64, top, pltpu.roll(low, 64, 1))
    halo_c[4] = t

    pl.semaphore_wait(barrier, 26)

    def remote(src, dst, send, recv, device):
        return pltpu.make_async_remote_copy(
            src_ref=src,
            dst_ref=dst,
            send_sem=send,
            recv_sem=recv,
            device_id=device,
            device_id_type=MESH,
        )

    def halo(offset):
        dx, dy, dz = offset
        plane = (dx + 1) * 3 + dy + 1
        slot = 8 - plane
        source = (pack_d, tc, pack_u)[dz + 1]
        target = (halo_r, halo_c, halo_l)[dz + 1]
        send = (hr_send, hc_send, hl_send)[dz + 1]
        recv = (hr_recv, hc_recv, hl_recv)[dz + 1]
        return remote(source, target.at[slot], send.at[plane], recv.at[slot], peer(*offset))

    for offset in OFFSETS:
        halo(offset).start()

    for copy in inputs[1:]:
        copy.wait()
    cells = lax.broadcasted_iota(jnp.int32, (48, WINDOW), 0)
    lane48 = lax.broadcasted_iota(jnp.int32, (48, LANES), 1)
    member = jnp.zeros((48, LANES), F32)
    for s in range(DEPTH):
        hit = jnp.where(members_ref[s : s + 1, :] == cells, 1.0, 0.0).astype(F32)
        some = jnp.max(hit, axis=1, keepdims=True)
        member = jnp.where(lane48 // L2 == s, some, member)
    mask[...] = member

    br = lax.broadcasted_iota(jnp.int32, (LANES, LANES), 0)
    bc = lax.broadcasted_iota(jnp.int32, (LANES, LANES), 1)
    blocks[...] = jnp.where(br // L2 == bc // L2, 1.0, 0.0).astype(BF16)

    deltas = jnp.concatenate(
        [turned4(table_ref[:, k * LANES : (k + 1) * LANES]) for k in range(8)], axis=0
    )
    code = jnp.zeros((L2, LANES), jnp.int32)
    for s in range(DEPTH):
        code = jnp.where(lane // L2 == s, s + 4 - species_ref[s], code)
    code = code % 4
    chosen = deltas
    for m in range(1, 4):
        chosen = jnp.where(code == m, pltpu.roll(deltas, L2 * m, 1), chosen)
    for s in range(DEPTH):
        dh, dl = split(jnp.where(lane // L2 == s, chosen, 0.0))
        rows = slice(s * L2, (s + 1) * L2)
        down = slice(LANES + s * L2, LANES + (s + 1) * L2)
        dbd[rows, :LANES] = dh
        dbd[rows, LANES:] = dl
        dbd[down, :LANES] = dh
        dbd[down, LANES:] = jnp.zeros((L2, LANES), BF16)

    w[:, 512:768, :] = jnp.zeros((2, 256, 2 * LANES), BF16)
    w[:, ROWS:, :] = jnp.zeros((2, PADDED - ROWS, 2 * LANES), BF16)
    th, tl = split(t)
    w[0, CENTRE * L2 : (CENTRE + 1) * L2, :LANES] = th
    w[0, CENTRE * L2 : (CENTRE + 1) * L2, LANES:] = tl
    sh[:, ROWS:] = jnp.zeros((ROWS, PADDED - ROWS), BF16)
    sl[:, ROWS:] = jnp.zeros((ROWS, PADDED - ROWS), BF16)

    for i in range(3):
        for j in range(3):
            rows_copy(3 * i + j).wait()
        rows = pl.ds(i * CHUNK, CHUNK)
        high, rest = split(sf[rows, :])
        sh[rows, :ROWS] = high
        sl[rows, :ROWS] = rest

    wide = w[0, 512:768, :]
    a = dot(sh[:, 512:768], wide)
    b = dot(sl[:, 512:768], wide[:, :LANES])
    image1[...] = a[:, :LANES] + (a[:, LANES:] + b)

    def windows_of(plane):
        dx, dy = plane // 3 - 1, plane % 3 - 1
        for dz in (-1, 0, 1):
            if (dx, dy, dz) != (0, 0, 0):
                halo((-dx, -dy, -dz)).wait_recv()
        centre = halo_c[plane]
        up, down = halo_l[plane], halo_r[plane]
        left = jnp.concatenate([pltpu.roll(up, 64, 1), up], axis=0)
        right = jnp.concatenate([down, pltpu.roll(down, 64, 1)], axis=0)
        windows = [
            pltpu.roll(jnp.where(lane < 64, centre, left), 64, 1),
            pltpu.roll(jnp.where(lane < 96, centre, left), 32, 1),
            centre,
            pltpu.roll(jnp.where(lane < 32, right, centre), 96, 1),
            pltpu.roll(jnp.where(lane < 64, right, centre), 64, 1),
        ]
        for k in range(5):
            cell = plane * 5 + k
            th, tl = split(windows[k] * mask[cell : cell + 1, :])
            tw[cell, :L2] = th
            tw[cell, L2:] = tl

    def blocks_times(image, cell, on):
        ih, il = split(image)
        wbd = jnp.concatenate(
            [
                jnp.concatenate([ih] * DEPTH, axis=0) * on,
                jnp.concatenate([il] * DEPTH, axis=0) * on,
            ],
            axis=1,
        )
        res = dot(tw[cell], wbd)
        x = res[:L2, :LANES] + (res[:L2, LANES:] + res[L2:, :LANES])
        return x + tc[...] if cell == CENTRE else x

    def both(x):
        return jnp.concatenate(split(x), axis=1)

    def images(rows, now):
        wide = w[now]
        a = dot(sh[rows, :], wide)
        b = dot(sl[rows, :], wide[:, :LANES])
        return a[:, :LANES] + (a[:, LANES:] + b)

    def sweep(now, later):
        image = images(slice(0, ROWS), now)
        on = blocks[...]
        for i in range(WINDOW):
            cell = cell_at(i)
            x = blocks_times(image[i * L2 : (i + 1) * L2], cell, on)
            w[later, cell * L2 : (cell + 1) * L2, :] = both(x)

    def last_sweep(now, planes):
        start = planes[0] * 160
        size = len(planes) * 160
        image = images(slice(start, start + size), now)
        on = blocks[...]
        columns = []
        for i in range(size // L2):
            cell = cell_at(planes[0] * 5 + i)
            x = blocks_times(image[i * L2 : (i + 1) * L2], cell, on)
            if cell == CENTRE:
                for k in range(8):
                    tau_ref[:, k * LANES : (k + 1) * LANES] = turned4(x[4 * k : 4 * k + 4])
            columns.append(both(x))
        r2 = dot(jnp.concatenate(columns, axis=0), dbd[...])
        r = r2[:, :LANES] + r2[:, LANES:]
        for j, position in enumerate(planes):
            plane = ORDER[position]
            rnat[plane * 160 : (plane + 1) * 160, :] = r[j * 160 : (j + 1) * 160]
            turned = []
            for k in range(5):
                at = j * 160 + k * L2
                block = r[at : at + L2]
                turned.append(pltpu.roll(block, (L2 * (k - 2)) % LANES, 1) if k != 2 else block)
            usend[plane, :16] = jnp.where(
                lane16 < 64, turned[4][:16], pltpu.roll(turned[4][16:], 64, 1)
            )
            usend[plane, 16:] = quarter(turned[3], 0)
            dsend[plane, :16] = jnp.where(
                lane16 >= 64, turned[0][:16], pltpu.roll(turned[0][16:], 64, 1)
            )
            dsend[plane, 16:] = quarter(turned[1], 3)
            target = mrecv if plane == 4 else msend
            target[plane, :32] = turned[2]
            target[plane, 32:64] = jnp.where(lane >= 64, turned[4], turned[0])
            target[plane, 64:96] = jnp.where(lane < 32, turned[1], turned[3])
            target[plane, 96:] = jnp.where(
                (lane16 >= 32) & (lane16 < 96), turned[1][:16], pltpu.roll(turned[1][16:], 64, 1)
            )
            for dz in (-1, 1, 0):
                if plane != 4 or dz:
                    pairs(plane, dz).start()

    def quarter(x, first):
        out = x[:8]
        for m in range(1, 4):
            moved = pltpu.roll(x[8 * m : 8 * m + 8], L2 * m, 1)
            out = jnp.where(lane8 // L2 == (first + m) % 4, moved, out)
        return out

    def unquarter(q):
        parts = [q] + [pltpu.roll(q, LANES - L2 * m, 1) for m in range(1, 4)]
        return jnp.concatenate(parts, axis=0)

    def unhalf(h):
        return jnp.concatenate([h, pltpu.roll(h, 64, 1)], axis=0)

    def pairs(plane, dz):
        dx, dy = plane // 3 - 1, plane % 3 - 1
        source = (dsend, msend, usend)[dz + 1]
        target = (drecv, mrecv, urecv)[dz + 1]
        send = (d_send, m_send, u_send)[dz + 1]
        recv = (d_recv, m_recv, u_recv)[dz + 1]
        return remote(
            source.at[plane], target.at[plane], send.at[plane], recv.at[plane], peer(dx, dy, dz)
        )

    for plane in ORDER[::-1]:
        windows_of(plane)
    on = blocks[...]
    for i in range(WINDOW):
        cell = cell_at(i)
        x = blocks_times(image1[i * L2 : (i + 1) * L2, :], cell, on)
        w[1, cell * L2 : (cell + 1) * L2, :] = both(x)

    @pl.loop(1, ITERS - 1)
    def _(n):
        now = lax.rem(n, 2)
        sweep(now, 1 - now)

    for planes in ((0, 1), (2, 3), (4, 5), (6, 7), (8,)):
        last_sweep((ITERS - 1) % 2, planes)

    rnat[ROWS:, :] = jnp.zeros((PADDED - ROWS, LANES), F32)

    @pl.loop(0, 3)
    def _(n):
        for m in range(4):
            i = 4 * n + m
            turned = rnat[pl.ds(pl.multiple_of(i * LANES, LANES), LANES), :].T
            for j in range(4):
                out = None
                for s in range(DEPTH):
                    part = turned[s * L2 : (s + 1) * L2]
                    shift = (L2 * (s - j)) % LANES
                    part = pltpu.roll(part, shift, 1) if shift else part
                    out = part if out is None else jnp.where(lane // L2 == s, part, out)
                rb[i * 4 + j] = out

    for plane in ORDER:
        for dz in (-1, 0, 1):
            if plane != 4 or dz:
                pairs(plane, dz).wait_recv()
        u2, u1 = unhalf(urecv[plane, :16]), unquarter(urecv[plane, 16:])
        d2, d1 = unhalf(drecv[plane, :16]), unquarter(drecv[plane, 16:])
        outer, inner = mrecv[plane, 32:64], mrecv[plane, 64:96]
        rest = unhalf(mrecv[plane, 96:])
        got = [
            jnp.where(lane < 64, outer, d2),
            jnp.where(lane < 32, inner, jnp.where(lane < 96, rest, d1)),
            mrecv[plane, :32],
            jnp.where(lane < 32, u1, inner),
            jnp.where(lane < 64, u2, outer),
        ]
        for k in range(5):
            cell = WINDOW - 1 - (plane * 5 + k)
            prow[cell : cell + 1, :] = jnp.sum(got[k] * rb[cell], axis=0, keepdims=True)

    prow[WINDOW:, :] = jnp.zeros((48 - WINDOW, LANES), F32)
    sr = lax.broadcasted_iota(jnp.int32, (8, LANES), 0)
    sc = lax.broadcasted_iota(jnp.int32, (8, LANES), 1)
    summed = jnp.where(sc // L2 == sr, 1.0, 0.0).astype(F32)
    sums = lax.dot_general(
        summed,
        prow[...],
        (((1,), (1,)), ((), ())),
        precision=lax.Precision.HIGHEST,
        preferred_element_type=F32,
    )
    pair_ref[...] = sums[:DEPTH, :WINDOW]

    for offset in OFFSETS:
        halo(offset).wait_send()
    for plane in ORDER:
        for dz in (-1, 0, 1):
            if plane != 4 or dz:
                pairs(plane, dz).wait_send()


def finish(tau_ref, pair_ref, tau_out, pair_out, sem):
    copies = (
        pltpu.make_async_copy(tau_ref, tau_out, sem.at[0]),
        pltpu.make_async_copy(pair_ref, pair_out, sem.at[1]),
    )
    for copy in copies:
        copy.start()
    for copy in copies:
        copy.wait()


def body(t_matrix, structure, species, members, delta_table):
    vmem = pl.BlockSpec(memory_space=pltpu.VMEM)
    dma = pltpu.SemaphoreType.DMA
    tau, pair = pl.pallas_call(
        kernel,
        out_shape=(
            jax.ShapeDtypeStruct((DEPTH, L2 * L2), F32),
            jax.ShapeDtypeStruct((DEPTH, WINDOW), F32),
        ),
        in_specs=[pl.BlockSpec(memory_space=pltpu.HBM)] * 5,
        out_specs=(vmem, vmem),
        scratch_shapes=[
            pltpu.VMEM((DEPTH, L2 * L2), F32),
            pltpu.SMEM((DEPTH,), jnp.int32),
            pltpu.VMEM((DEPTH, WINDOW), jnp.int32),
            pltpu.VMEM((SPECIES, L2 * L2), F32),
            pltpu.VMEM((ROWS, ROWS), F32),
            pltpu.VMEM((ROWS, PADDED), BF16),
            pltpu.VMEM((ROWS, PADDED), BF16),
            pltpu.VMEM((2, PADDED, 2 * LANES), BF16),
            pltpu.VMEM((WINDOW, 2 * L2, LANES), BF16),
            pltpu.VMEM((9, L2, LANES), F32),
            pltpu.VMEM((9, L2 // 2, LANES), F32),
            pltpu.VMEM((9, L2 // 2, LANES), F32),
            pltpu.VMEM((L2 // 2, LANES), F32),
            pltpu.VMEM((L2 // 2, LANES), F32),
            pltpu.VMEM((48, LANES), F32),
            pltpu.VMEM((LANES, LANES), BF16),
            pltpu.VMEM((2 * LANES, 2 * LANES), BF16),
            pltpu.VMEM((L2, LANES), F32),
            pltpu.VMEM((ROWS, LANES), F32),
            pltpu.VMEM((PADDED, LANES), F32),
            pltpu.VMEM((48, L2, LANES), F32),
            pltpu.VMEM((48, LANES), F32),
            pltpu.VMEM((9, 112, LANES), F32),
            pltpu.VMEM((9, 24, LANES), F32),
            pltpu.VMEM((9, 24, LANES), F32),
            pltpu.VMEM((9, 112, LANES), F32),
            pltpu.VMEM((9, 24, LANES), F32),
            pltpu.VMEM((9, 24, LANES), F32),
        ]
        + [dma((4,))]
        + [dma((9,))] * 13,
        compiler_params=pltpu.CompilerParams(
            collective_id=0, has_side_effects=True, vmem_limit_bytes=50 << 20
        ),
    )(
        *(
            pltpu.with_memory_space_constraint(x, pltpu.HBM)
            for x in (
                t_matrix.reshape(DEPTH, L2 * L2),
                structure,
                species.reshape(DEPTH),
                members.reshape(DEPTH, WINDOW),
                delta_table,
            )
        )
    )
    anywhere = pl.BlockSpec(memory_space=pl.ANY)
    tau, pair = pl.pallas_call(
        finish,
        out_shape=(
            jax.ShapeDtypeStruct((DEPTH, L2 * L2), F32),
            jax.ShapeDtypeStruct((DEPTH, WINDOW), F32),
        ),
        in_specs=[anywhere] * 2,
        out_specs=(anywhere,) * 2,
        scratch_shapes=[dma((2,))],
        compiler_params=pltpu.CompilerParams(vmem_limit_bytes=16 << 20),
    )(tau, pair)
    return tau.reshape(1, 1, 1, DEPTH, L2 * L2), pair.reshape(1, 1, DEPTH, WINDOW)


def solution(mesh):
    placed = (
        P(None, "gx", "gy", "gz", None),
        P(),
        P("gx", "gy", "gz"),
        P("gx", "gy", "gz", None),
        P(),
    )
    return jax.shard_map(
        body,
        mesh=mesh,
        in_specs=placed,
        out_specs=(P(None, "gx", "gy", "gz", None), P("gx", "gy", "gz", None)),
        check_vma=False,
    )
```

```python
import jax
import jax.numpy as jnp
from jax import lax
from jax.experimental import pallas as pl
from jax.experimental.pallas import tpu as pltpu
from jax.sharding import PartitionSpec as P

L2 = 32
WINDOW = 45
ITERS = 4
SPECIES = 4
DEPTH = 4
LANES = DEPTH * L2
ROWS = WINDOW * L2
PADDED = 1536
CHUNK = ROWS // 3
CELLS = WINDOW // 3
CENTRE = WINDOW // 2
F32 = jnp.float32
BF16 = jnp.bfloat16
MESH = pl.DeviceIdType.MESH
ORDER = (0, 8, 2, 6, 3, 5, 1, 7, 4)
OFFSETS = sorted(
    [(x, y, z) for x in (-1, 0, 1) for y in (-1, 0, 1) for z in (-1, 0, 1) if x or y or z],
    key=lambda o: -(abs(o[0]) + abs(o[1]) + abs(o[2])),
)


def cell_at(position):
    return ORDER[position // 5] * 5 + position % 5


def split(x):
    high = x.astype(BF16)
    return high, (x - high.astype(F32)).astype(BF16)


def dot(a, b):
    return jnp.dot(a, b, preferred_element_type=F32)


def turned4(p):
    q = jnp.concatenate([p, p], axis=0)
    row = lax.broadcasted_iota(jnp.int32, (8, LANES), 0)
    block = lax.broadcasted_iota(jnp.int32, (8, LANES), 1) // L2
    out = q
    for d in range(1, 4):
        moved = pltpu.roll(pltpu.roll(q, L2 * d, 1), 8 - d, 0)
        out = jnp.where((block - row + 8) % 4 == d, moved, out)
    return out[:4]


def kernel(
    t_hbm,
    s_hbm,
    species_hbm,
    members_hbm,
    table_hbm,
    tau_ref,
    pair_ref,
    t_ref,
    species_ref,
    members_ref,
    table_ref,
    sf,
    sh,
    sl,
    w,
    tw,
    halo_c,
    halo_l,
    halo_r,
    pack_u,
    pack_d,
    mask,
    blocks,
    dbd,
    tc,
    image1,
    rnat,
    rb,
    prow,
    msend,
    usend,
    dsend,
    mrecv,
    urecv,
    drecv,
    in_sem,
    s_sem,
    hc_send,
    hl_send,
    hr_send,
    hc_recv,
    hl_recv,
    hr_recv,
    m_send,
    u_send,
    d_send,
    m_recv,
    u_recv,
    d_recv,
):
    gx, gy, gz = lax.axis_index("gx"), lax.axis_index("gy"), lax.axis_index("gz")
    nx, ny, nz = lax.axis_size("gx"), lax.axis_size("gy"), lax.axis_size("gz")

    xs = (lax.rem(gx + nx - 1, nx), gx, lax.rem(gx + 1, nx))
    ys = (lax.rem(gy + ny - 1, ny), gy, lax.rem(gy + 1, ny))
    zs = (lax.rem(gz + nz - 1, nz), gz, lax.rem(gz + 1, nz))

    def peer(dx, dy, dz):
        return (xs[dx + 1], ys[dy + 1], zs[dz + 1])

    inputs = [
        pltpu.make_async_copy(source, target, in_sem.at[i])
        for i, (source, target) in enumerate(
            (
                (t_hbm, t_ref),
                (species_hbm, species_ref),
                (members_hbm, members_ref),
                (table_hbm, table_ref),
            )
        )
    ]
    for copy in inputs:
        copy.start()

    barrier = pltpu.get_barrier_semaphore()
    for offset in OFFSETS:
        pl.semaphore_signal(barrier, inc=1, device_id=peer(*offset), device_id_type=MESH)

    def rows_copy(i):
        return pltpu.make_async_copy(
            s_hbm.at[0, pl.ds(ORDER[i] * 160, 160), :],
            sf.at[pl.ds(i * 160, 160), :],
            s_sem.at[i],
        )

    for i in range(9):
        rows_copy(i).start()

    lane = lax.broadcasted_iota(jnp.int32, (L2, LANES), 1)
    lane8 = lax.broadcasted_iota(jnp.int32, (8, LANES), 1)
    lane16 = lax.broadcasted_iota(jnp.int32, (L2 // 2, LANES), 1)
    inputs[0].wait()
    for k in range(8):
        tc[4 * k : 4 * k + 4, :] = turned4(t_ref[:, k * LANES : (k + 1) * LANES])
    t = tc[...]
    top, low = t[: L2 // 2], t[L2 // 2 :]
    pack_u[...] = jnp.where(lane16 < 64, pltpu.roll(top, 64, 1), low)
    pack_d[...] = jnp.where(lane16 < 64, top, pltpu.roll(low, 64, 1))
    halo_c[4] = t

    pl.semaphore_wait(barrier, 26)

    def remote(src, dst, send, recv, device):
        return pltpu.make_async_remote_copy(
            src_ref=src,
            dst_ref=dst,
            send_sem=send,
            recv_sem=recv,
            device_id=device,
            device_id_type=MESH,
        )

    def halo(offset):
        dx, dy, dz = offset
        plane = (dx + 1) * 3 + dy + 1
        slot = 8 - plane
        source = (pack_d, tc, pack_u)[dz + 1]
        target = (halo_r, halo_c, halo_l)[dz + 1]
        send = (hr_send, hc_send, hl_send)[dz + 1]
        recv = (hr_recv, hc_recv, hl_recv)[dz + 1]
        return remote(source, target.at[slot], send.at[plane], recv.at[slot], peer(*offset))

    for offset in OFFSETS:
        halo(offset).start()

    for copy in inputs[1:]:
        copy.wait()
    cells = lax.broadcasted_iota(jnp.int32, (48, WINDOW), 0)
    lane48 = lax.broadcasted_iota(jnp.int32, (48, LANES), 1)
    member = jnp.zeros((48, LANES), F32)
    for s in range(DEPTH):
        hit = jnp.where(members_ref[s : s + 1, :] == cells, 1.0, 0.0).astype(F32)
        some = jnp.max(hit, axis=1, keepdims=True)
        member = jnp.where(lane48 // L2 == s, some, member)
    mask[...] = member

    br = lax.broadcasted_iota(jnp.int32, (LANES, LANES), 0)
    bc = lax.broadcasted_iota(jnp.int32, (LANES, LANES), 1)
    blocks[...] = jnp.where(br // L2 == bc // L2, 1.0, 0.0).astype(BF16)

    deltas = jnp.concatenate(
        [turned4(table_ref[:, k * LANES : (k + 1) * LANES]) for k in range(8)], axis=0
    )
    code = jnp.zeros((L2, LANES), jnp.int32)
    for s in range(DEPTH):
        code = jnp.where(lane // L2 == s, s + 4 - species_ref[s], code)
    code = code % 4
    chosen = deltas
    for m in range(1, 4):
        chosen = jnp.where(code == m, pltpu.roll(deltas, L2 * m, 1), chosen)
    for s in range(DEPTH):
        dh, dl = split(jnp.where(lane // L2 == s, chosen, 0.0))
        rows = slice(s * L2, (s + 1) * L2)
        down = slice(LANES + s * L2, LANES + (s + 1) * L2)
        dbd[rows, :LANES] = dh
        dbd[rows, LANES:] = dl
        dbd[down, :LANES] = dh
        dbd[down, LANES:] = jnp.zeros((L2, LANES), BF16)

    w[:, 512:768, :] = jnp.zeros((2, 256, 2 * LANES), BF16)
    w[:, ROWS:, :] = jnp.zeros((2, PADDED - ROWS, 2 * LANES), BF16)
    rnat[ROWS:, :] = jnp.zeros((PADDED - ROWS, LANES), F32)
    prow[WINDOW:, :] = jnp.zeros((48 - WINDOW, LANES), F32)
    th, tl = split(t)
    w[0, CENTRE * L2 : (CENTRE + 1) * L2, :LANES] = th
    w[0, CENTRE * L2 : (CENTRE + 1) * L2, LANES:] = tl
    sh[:, ROWS:] = jnp.zeros((ROWS, PADDED - ROWS), BF16)
    sl[:, ROWS:] = jnp.zeros((ROWS, PADDED - ROWS), BF16)

    for i in range(3):
        for j in range(3):
            rows_copy(3 * i + j).wait()
        rows = pl.ds(i * CHUNK, CHUNK)
        high, rest = split(sf[rows, :])
        sh[rows, :ROWS] = high
        sl[rows, :ROWS] = rest

    wide = w[0, 512:768, :]
    a = dot(sh[:, 512:768], wide)
    b = dot(sl[:, 512:768], wide[:, :LANES])
    image1[...] = a[:, :LANES] + (a[:, LANES:] + b)

    def windows_of(plane):
        dx, dy = plane // 3 - 1, plane % 3 - 1
        for dz in (-1, 0, 1):
            if (dx, dy, dz) != (0, 0, 0):
                halo((-dx, -dy, -dz)).wait_recv()
        centre = halo_c[plane]
        up, down = halo_l[plane], halo_r[plane]
        left = jnp.concatenate([pltpu.roll(up, 64, 1), up], axis=0)
        right = jnp.concatenate([down, pltpu.roll(down, 64, 1)], axis=0)
        windows = [
            pltpu.roll(jnp.where(lane < 64, centre, left), 64, 1),
            pltpu.roll(jnp.where(lane < 96, centre, left), 32, 1),
            centre,
            pltpu.roll(jnp.where(lane < 32, right, centre), 96, 1),
            pltpu.roll(jnp.where(lane < 64, right, centre), 64, 1),
        ]
        for k in range(5):
            cell = plane * 5 + k
            th, tl = split(windows[k] * mask[cell : cell + 1, :])
            tw[cell, :L2] = th
            tw[cell, L2:] = tl

    def blocks_times(image, cell, on):
        ih, il = split(image)
        wbd = jnp.concatenate(
            [
                jnp.concatenate([ih] * DEPTH, axis=0) * on,
                jnp.concatenate([il] * DEPTH, axis=0) * on,
            ],
            axis=1,
        )
        res = dot(tw[cell], wbd)
        x = res[:L2, :LANES] + (res[:L2, LANES:] + res[L2:, :LANES])
        return x + tc[...] if cell == CENTRE else x

    def both(x):
        return jnp.concatenate(split(x), axis=1)

    def images(rows, now):
        wide = w[now]
        a = dot(sh[rows, :], wide)
        b = dot(sl[rows, :], wide[:, :LANES])
        return a[:, :LANES] + (a[:, LANES:] + b)

    def sweep(now, later):
        image = images(slice(0, ROWS), now)
        on = blocks[...]
        for i in range(WINDOW):
            cell = cell_at(i)
            x = blocks_times(image[i * L2 : (i + 1) * L2], cell, on)
            w[later, cell * L2 : (cell + 1) * L2, :] = both(x)

    def last_sweep(now, planes):
        start = planes[0] * 160
        size = len(planes) * 160
        image = images(slice(start, start + size), now)
        on = blocks[...]
        columns = []
        for i in range(size // L2):
            cell = cell_at(planes[0] * 5 + i)
            x = blocks_times(image[i * L2 : (i + 1) * L2], cell, on)
            if cell == CENTRE:
                for k in range(8):
                    tau_ref[:, k * LANES : (k + 1) * LANES] = turned4(x[4 * k : 4 * k + 4])
            columns.append(both(x))
        r2 = dot(jnp.concatenate(columns, axis=0), dbd[...])
        r = r2[:, :LANES] + r2[:, LANES:]
        for j, position in enumerate(planes):
            plane = ORDER[position]
            rnat[plane * 160 : (plane + 1) * 160, :] = r[j * 160 : (j + 1) * 160]
            turned = []
            for k in range(5):
                at = j * 160 + k * L2
                block = r[at : at + L2]
                turned.append(pltpu.roll(block, (L2 * (k - 2)) % LANES, 1) if k != 2 else block)
            usend[plane, :16] = jnp.where(
                lane16 < 64, turned[4][:16], pltpu.roll(turned[4][16:], 64, 1)
            )
            usend[plane, 16:] = quarter(turned[3], 0)
            dsend[plane, :16] = jnp.where(
                lane16 >= 64, turned[0][:16], pltpu.roll(turned[0][16:], 64, 1)
            )
            dsend[plane, 16:] = quarter(turned[1], 3)
            target = mrecv if plane == 4 else msend
            target[plane, :32] = turned[2]
            target[plane, 32:64] = jnp.where(lane >= 64, turned[4], turned[0])
            target[plane, 64:96] = jnp.where(lane < 32, turned[1], turned[3])
            target[plane, 96:] = jnp.where(
                (lane16 >= 32) & (lane16 < 96), turned[1][:16], pltpu.roll(turned[1][16:], 64, 1)
            )
            for dz in (-1, 1, 0):
                if plane != 4 or dz:
                    pairs(plane, dz).start()

    def quarter(x, first):
        out = x[:8]
        for m in range(1, 4):
            moved = pltpu.roll(x[8 * m : 8 * m + 8], L2 * m, 1)
            out = jnp.where(lane8 // L2 == (first + m) % 4, moved, out)
        return out

    def unquarter(q):
        parts = [q] + [pltpu.roll(q, LANES - L2 * m, 1) for m in range(1, 4)]
        return jnp.concatenate(parts, axis=0)

    def unhalf(h):
        return jnp.concatenate([h, pltpu.roll(h, 64, 1)], axis=0)

    def pairs(plane, dz):
        dx, dy = plane // 3 - 1, plane % 3 - 1
        source = (dsend, msend, usend)[dz + 1]
        target = (drecv, mrecv, urecv)[dz + 1]
        send = (d_send, m_send, u_send)[dz + 1]
        recv = (d_recv, m_recv, u_recv)[dz + 1]
        return remote(
            source.at[plane], target.at[plane], send.at[plane], recv.at[plane], peer(dx, dy, dz)
        )

    for plane in ORDER[::-1]:
        windows_of(plane)
    on = blocks[...]
    for i in range(WINDOW):
        cell = cell_at(i)
        x = blocks_times(image1[i * L2 : (i + 1) * L2, :], cell, on)
        w[1, cell * L2 : (cell + 1) * L2, :] = both(x)

    @pl.loop(1, ITERS - 1)
    def _(n):
        now = lax.rem(n, 2)
        sweep(now, 1 - now)

    for planes in ((0, 1, 2), (3, 4, 5), (6, 7, 8)):
        last_sweep((ITERS - 1) % 2, planes)


    @pl.loop(0, 3)
    def _(n):
        for m in range(4):
            i = 4 * n + m
            turned = rnat[pl.ds(pl.multiple_of(i * LANES, LANES), LANES), :].T
            for j in range(4):
                out = None
                for s in range(DEPTH):
                    part = turned[s * L2 : (s + 1) * L2]
                    shift = (L2 * (s - j)) % LANES
                    part = pltpu.roll(part, shift, 1) if shift else part
                    out = part if out is None else jnp.where(lane // L2 == s, part, out)
                rb[i * 4 + j] = out

    for plane in ORDER:
        for dz in (-1, 0, 1):
            if plane != 4 or dz:
                pairs(plane, dz).wait_recv()
        u2, u1 = unhalf(urecv[plane, :16]), unquarter(urecv[plane, 16:])
        d2, d1 = unhalf(drecv[plane, :16]), unquarter(drecv[plane, 16:])
        outer, inner = mrecv[plane, 32:64], mrecv[plane, 64:96]
        rest = unhalf(mrecv[plane, 96:])
        got = [
            jnp.where(lane < 64, outer, d2),
            jnp.where(lane < 32, inner, jnp.where(lane < 96, rest, d1)),
            mrecv[plane, :32],
            jnp.where(lane < 32, u1, inner),
            jnp.where(lane < 64, u2, outer),
        ]
        for k in range(5):
            cell = WINDOW - 1 - (plane * 5 + k)
            prow[cell : cell + 1, :] = jnp.sum(got[k] * rb[cell], axis=0, keepdims=True)

    sr = lax.broadcasted_iota(jnp.int32, (8, LANES), 0)
    sc = lax.broadcasted_iota(jnp.int32, (8, LANES), 1)
    summed = jnp.where(sc // L2 == sr, 1.0, 0.0).astype(F32)
    sums = lax.dot_general(
        summed,
        prow[...],
        (((1,), (1,)), ((), ())),
        precision=lax.Precision.HIGHEST,
        preferred_element_type=F32,
    )
    pair_ref[...] = sums[:DEPTH, :WINDOW]

    for offset in OFFSETS:
        halo(offset).wait_send()
    for plane in ORDER:
        for dz in (-1, 0, 1):
            if plane != 4 or dz:
                pairs(plane, dz).wait_send()


def finish(tau_ref, pair_ref, tau_out, pair_out, sem):
    copies = (
        pltpu.make_async_copy(tau_ref, tau_out, sem.at[0]),
        pltpu.make_async_copy(pair_ref, pair_out, sem.at[1]),
    )
    for copy in copies:
        copy.start()
    for copy in copies:
        copy.wait()


def body(t_matrix, structure, species, members, delta_table):
    vmem = pl.BlockSpec(memory_space=pltpu.VMEM)
    dma = pltpu.SemaphoreType.DMA
    tau, pair = pl.pallas_call(
        kernel,
        out_shape=(
            jax.ShapeDtypeStruct((DEPTH, L2 * L2), F32),
            jax.ShapeDtypeStruct((DEPTH, WINDOW), F32),
        ),
        in_specs=[pl.BlockSpec(memory_space=pltpu.HBM)] * 5,
        out_specs=(vmem, vmem),
        scratch_shapes=[
            pltpu.VMEM((DEPTH, L2 * L2), F32),
            pltpu.SMEM((DEPTH,), jnp.int32),
            pltpu.VMEM((DEPTH, WINDOW), jnp.int32),
            pltpu.VMEM((SPECIES, L2 * L2), F32),
            pltpu.VMEM((ROWS, ROWS), F32),
            pltpu.VMEM((ROWS, PADDED), BF16),
            pltpu.VMEM((ROWS, PADDED), BF16),
            pltpu.VMEM((2, PADDED, 2 * LANES), BF16),
            pltpu.VMEM((WINDOW, 2 * L2, LANES), BF16),
            pltpu.VMEM((9, L2, LANES), F32),
            pltpu.VMEM((9, L2 // 2, LANES), F32),
            pltpu.VMEM((9, L2 // 2, LANES), F32),
            pltpu.VMEM((L2 // 2, LANES), F32),
            pltpu.VMEM((L2 // 2, LANES), F32),
            pltpu.VMEM((48, LANES), F32),
            pltpu.VMEM((LANES, LANES), BF16),
            pltpu.VMEM((2 * LANES, 2 * LANES), BF16),
            pltpu.VMEM((L2, LANES), F32),
            pltpu.VMEM((ROWS, LANES), F32),
            pltpu.VMEM((PADDED, LANES), F32),
            pltpu.VMEM((48, L2, LANES), F32),
            pltpu.VMEM((48, LANES), F32),
            pltpu.VMEM((9, 112, LANES), F32),
            pltpu.VMEM((9, 24, LANES), F32),
            pltpu.VMEM((9, 24, LANES), F32),
            pltpu.VMEM((9, 112, LANES), F32),
            pltpu.VMEM((9, 24, LANES), F32),
            pltpu.VMEM((9, 24, LANES), F32),
        ]
        + [dma((4,))]
        + [dma((9,))] * 13,
        compiler_params=pltpu.CompilerParams(
            collective_id=0, has_side_effects=True, vmem_limit_bytes=50 << 20
        ),
    )(
        *(
            pltpu.with_memory_space_constraint(x, pltpu.HBM)
            for x in (
                t_matrix.reshape(DEPTH, L2 * L2),
                structure,
                species.reshape(DEPTH),
                members.reshape(DEPTH, WINDOW),
                delta_table,
            )
        )
    )
    anywhere = pl.BlockSpec(memory_space=pl.ANY)
    tau, pair = pl.pallas_call(
        finish,
        out_shape=(
            jax.ShapeDtypeStruct((DEPTH, L2 * L2), F32),
            jax.ShapeDtypeStruct((DEPTH, WINDOW), F32),
        ),
        in_specs=[anywhere] * 2,
        out_specs=(anywhere,) * 2,
        scratch_shapes=[dma((2,))],
        compiler_params=pltpu.CompilerParams(vmem_limit_bytes=16 << 20),
    )(tau, pair)
    return tau.reshape(1, 1, 1, DEPTH, L2 * L2), pair.reshape(1, 1, DEPTH, WINDOW)


def solution(mesh):
    placed = (
        P(None, "gx", "gy", "gz", None),
        P(),
        P("gx", "gy", "gz"),
        P("gx", "gy", "gz", None),
        P(),
    )
    return jax.shard_map(
        body,
        mesh=mesh,
        in_specs=placed,
        out_specs=(P(None, "gx", "gy", "gz", None), P("gx", "gy", "gz", None)),
        check_vma=False,
    )
```

```python
import jax
import jax.numpy as jnp
from jax import lax
from jax.experimental import pallas as pl
from jax.experimental.pallas import tpu as pltpu
from jax.sharding import PartitionSpec as P

L2 = 32
WINDOW = 45
ITERS = 4
SPECIES = 4
DEPTH = 4
LANES = DEPTH * L2
ROWS = WINDOW * L2
PADDED = 1536
CHUNK = ROWS // 3
CELLS = WINDOW // 3
CENTRE = WINDOW // 2
F32 = jnp.float32
BF16 = jnp.bfloat16
MESH = pl.DeviceIdType.MESH
ORDER = (0, 8, 2, 6, 3, 5, 1, 7, 4)
OFFSETS = sorted(
    [(x, y, z) for x in (-1, 0, 1) for y in (-1, 0, 1) for z in (-1, 0, 1) if x or y or z],
    key=lambda o: -(abs(o[0]) + abs(o[1]) + abs(o[2])),
)


def cell_at(position):
    return ORDER[position // 5] * 5 + position % 5


def split(x):
    high = x.astype(BF16)
    return high, (x - high.astype(F32)).astype(BF16)


def dot(a, b):
    return jnp.dot(a, b, preferred_element_type=F32)


def turned4(p):
    q = jnp.concatenate([p, p], axis=0)
    row = lax.broadcasted_iota(jnp.int32, (8, LANES), 0)
    block = lax.broadcasted_iota(jnp.int32, (8, LANES), 1) // L2
    out = q
    for d in range(1, 4):
        moved = pltpu.roll(pltpu.roll(q, L2 * d, 1), 8 - d, 0)
        out = jnp.where((block - row + 8) % 4 == d, moved, out)
    return out[:4]


def kernel(
    t_hbm,
    s_hbm,
    species_hbm,
    members_hbm,
    table_hbm,
    tau_ref,
    pair_ref,
    t_ref,
    species_ref,
    members_ref,
    table_ref,
    sf,
    sh,
    sl,
    w,
    tw,
    halo_c,
    halo_l,
    halo_r,
    pack_u,
    pack_d,
    mask,
    blocks,
    dbd,
    tc,
    image1,
    spread1,
    rnat,
    rb,
    prow,
    msend,
    usend,
    dsend,
    mrecv,
    urecv,
    drecv,
    in_sem,
    s_sem,
    hc_send,
    hl_send,
    hr_send,
    hc_recv,
    hl_recv,
    hr_recv,
    m_send,
    u_send,
    d_send,
    m_recv,
    u_recv,
    d_recv,
):
    gx, gy, gz = lax.axis_index("gx"), lax.axis_index("gy"), lax.axis_index("gz")
    nx, ny, nz = lax.axis_size("gx"), lax.axis_size("gy"), lax.axis_size("gz")

    xs = (lax.rem(gx + nx - 1, nx), gx, lax.rem(gx + 1, nx))
    ys = (lax.rem(gy + ny - 1, ny), gy, lax.rem(gy + 1, ny))
    zs = (lax.rem(gz + nz - 1, nz), gz, lax.rem(gz + 1, nz))

    def peer(dx, dy, dz):
        return (xs[dx + 1], ys[dy + 1], zs[dz + 1])

    inputs = [
        pltpu.make_async_copy(source, target, in_sem.at[i])
        for i, (source, target) in enumerate(
            (
                (t_hbm, t_ref),
                (species_hbm, species_ref),
                (members_hbm, members_ref),
                (table_hbm, table_ref),
            )
        )
    ]
    for copy in inputs:
        copy.start()

    barrier = pltpu.get_barrier_semaphore()
    for offset in OFFSETS:
        pl.semaphore_signal(barrier, inc=1, device_id=peer(*offset), device_id_type=MESH)

    def rows_copy(i):
        return pltpu.make_async_copy(
            s_hbm.at[0, pl.ds(ORDER[i] * 160, 160), :],
            sf.at[pl.ds(i * 160, 160), :],
            s_sem.at[i],
        )

    for i in range(9):
        rows_copy(i).start()

    lane = lax.broadcasted_iota(jnp.int32, (L2, LANES), 1)
    lane8 = lax.broadcasted_iota(jnp.int32, (8, LANES), 1)
    lane16 = lax.broadcasted_iota(jnp.int32, (L2 // 2, LANES), 1)
    inputs[0].wait()
    for k in range(8):
        tc[4 * k : 4 * k + 4, :] = turned4(t_ref[:, k * LANES : (k + 1) * LANES])
    t = tc[...]
    top, low = t[: L2 // 2], t[L2 // 2 :]
    pack_u[...] = jnp.where(lane16 < 64, pltpu.roll(top, 64, 1), low)
    pack_d[...] = jnp.where(lane16 < 64, top, pltpu.roll(low, 64, 1))
    halo_c[4] = t

    pl.semaphore_wait(barrier, 26)

    def remote(src, dst, send, recv, device):
        return pltpu.make_async_remote_copy(
            src_ref=src,
            dst_ref=dst,
            send_sem=send,
            recv_sem=recv,
            device_id=device,
            device_id_type=MESH,
        )

    def halo(offset):
        dx, dy, dz = offset
        plane = (dx + 1) * 3 + dy + 1
        slot = 8 - plane
        source = (pack_d, tc, pack_u)[dz + 1]
        target = (halo_r, halo_c, halo_l)[dz + 1]
        send = (hr_send, hc_send, hl_send)[dz + 1]
        recv = (hr_recv, hc_recv, hl_recv)[dz + 1]
        return remote(source, target.at[slot], send.at[plane], recv.at[slot], peer(*offset))

    for offset in OFFSETS:
        halo(offset).start()

    for copy in inputs[1:]:
        copy.wait()
    cells = lax.broadcasted_iota(jnp.int32, (48, WINDOW), 0)
    lane48 = lax.broadcasted_iota(jnp.int32, (48, LANES), 1)
    member = jnp.zeros((48, LANES), F32)
    for s in range(DEPTH):
        hit = jnp.where(members_ref[s : s + 1, :] == cells, 1.0, 0.0).astype(F32)
        some = jnp.max(hit, axis=1, keepdims=True)
        member = jnp.where(lane48 // L2 == s, some, member)
    mask[...] = member

    br = lax.broadcasted_iota(jnp.int32, (LANES, LANES), 0)
    bc = lax.broadcasted_iota(jnp.int32, (LANES, LANES), 1)
    blocks[...] = jnp.where(br // L2 == bc // L2, 1.0, 0.0).astype(BF16)

    deltas = jnp.concatenate(
        [turned4(table_ref[:, k * LANES : (k + 1) * LANES]) for k in range(8)], axis=0
    )
    code = jnp.zeros((L2, LANES), jnp.int32)
    for s in range(DEPTH):
        code = jnp.where(lane // L2 == s, s + 4 - species_ref[s], code)
    code = code % 4
    chosen = deltas
    for m in range(1, 4):
        chosen = jnp.where(code == m, pltpu.roll(deltas, L2 * m, 1), chosen)
    for s in range(DEPTH):
        dh, dl = split(jnp.where(lane // L2 == s, chosen, 0.0))
        rows = slice(s * L2, (s + 1) * L2)
        down = slice(LANES + s * L2, LANES + (s + 1) * L2)
        dbd[rows, :LANES] = dh
        dbd[rows, LANES:] = dl
        dbd[down, :LANES] = dh
        dbd[down, LANES:] = jnp.zeros((L2, LANES), BF16)

    w[:, 512:768, :] = jnp.zeros((2, 256, 2 * LANES), BF16)
    w[:, ROWS:, :] = jnp.zeros((2, PADDED - ROWS, 2 * LANES), BF16)
    rnat[ROWS:, :] = jnp.zeros((PADDED - ROWS, LANES), F32)
    prow[WINDOW:, :] = jnp.zeros((48 - WINDOW, LANES), F32)
    th, tl = split(t)
    w[0, CENTRE * L2 : (CENTRE + 1) * L2, :LANES] = th
    w[0, CENTRE * L2 : (CENTRE + 1) * L2, LANES:] = tl
    sh[:, ROWS:] = jnp.zeros((ROWS, PADDED - ROWS), BF16)
    sl[:, ROWS:] = jnp.zeros((ROWS, PADDED - ROWS), BF16)

    for i in range(3):
        for j in range(3):
            rows_copy(3 * i + j).wait()
        rows = pl.ds(i * CHUNK, CHUNK)
        high, rest = split(sf[rows, :])
        sh[rows, :ROWS] = high
        sl[rows, :ROWS] = rest

    wide = w[0, 512:768, :]
    a = dot(sh[:, 512:768], wide)
    b = dot(sl[:, 512:768], wide[:, :LANES])
    image1[...] = a[:, :LANES] + (a[:, LANES:] + b)

    def windows_of(plane):
        dx, dy = plane // 3 - 1, plane % 3 - 1
        for dz in (-1, 0, 1):
            if (dx, dy, dz) != (0, 0, 0):
                halo((-dx, -dy, -dz)).wait_recv()
        centre = halo_c[plane]
        up, down = halo_l[plane], halo_r[plane]
        left = jnp.concatenate([pltpu.roll(up, 64, 1), up], axis=0)
        right = jnp.concatenate([down, pltpu.roll(down, 64, 1)], axis=0)
        windows = [
            pltpu.roll(jnp.where(lane < 64, centre, left), 64, 1),
            pltpu.roll(jnp.where(lane < 96, centre, left), 32, 1),
            centre,
            pltpu.roll(jnp.where(lane < 32, right, centre), 96, 1),
            pltpu.roll(jnp.where(lane < 64, right, centre), 64, 1),
        ]
        for k in range(5):
            cell = plane * 5 + k
            th, tl = split(windows[k] * mask[cell : cell + 1, :])
            tw[cell, :L2] = th
            tw[cell, L2:] = tl

    def spread(image, on):
        ih, il = split(image)
        return jnp.concatenate(
            [
                jnp.concatenate([ih] * DEPTH, axis=0) * on,
                jnp.concatenate([il] * DEPTH, axis=0) * on,
            ],
            axis=1,
        )

    def blocks_times(image, cell, on):
        return times(spread(image, on), cell)

    def times(wide, cell):
        res = dot(tw[cell], wide)
        x = res[:L2, :LANES] + (res[:L2, LANES:] + res[L2:, :LANES])
        return x + tc[...] if cell == CENTRE else x

    def both(x):
        return jnp.concatenate(split(x), axis=1)

    def images(rows, now):
        wide = w[now]
        a = dot(sh[rows, :], wide)
        b = dot(sl[rows, :], wide[:, :LANES])
        return a[:, :LANES] + (a[:, LANES:] + b)

    def sweep(now, later):
        image = images(slice(0, ROWS), now)
        on = blocks[...]
        for i in range(WINDOW):
            cell = cell_at(i)
            x = blocks_times(image[i * L2 : (i + 1) * L2], cell, on)
            w[later, cell * L2 : (cell + 1) * L2, :] = both(x)

    def last_sweep(now, planes):
        start = planes[0] * 160
        size = len(planes) * 160
        image = images(slice(start, start + size), now)
        on = blocks[...]
        columns = []
        for i in range(size // L2):
            cell = cell_at(planes[0] * 5 + i)
            x = blocks_times(image[i * L2 : (i + 1) * L2], cell, on)
            if cell == CENTRE:
                for k in range(8):
                    tau_ref[:, k * LANES : (k + 1) * LANES] = turned4(x[4 * k : 4 * k + 4])
            columns.append(both(x))
        r2 = dot(jnp.concatenate(columns, axis=0), dbd[...])
        r = r2[:, :LANES] + r2[:, LANES:]
        for j, position in enumerate(planes):
            plane = ORDER[position]
            rnat[plane * 160 : (plane + 1) * 160, :] = r[j * 160 : (j + 1) * 160]
            turned = []
            for k in range(5):
                at = j * 160 + k * L2
                block = r[at : at + L2]
                turned.append(pltpu.roll(block, (L2 * (k - 2)) % LANES, 1) if k != 2 else block)
            usend[plane, :16] = jnp.where(
                lane16 < 64, turned[4][:16], pltpu.roll(turned[4][16:], 64, 1)
            )
            usend[plane, 16:] = quarter(turned[3], 0)
            dsend[plane, :16] = jnp.where(
                lane16 >= 64, turned[0][:16], pltpu.roll(turned[0][16:], 64, 1)
            )
            dsend[plane, 16:] = quarter(turned[1], 3)
            target = mrecv if plane == 4 else msend
            target[plane, :32] = turned[2]
            target[plane, 32:64] = jnp.where(lane >= 64, turned[4], turned[0])
            target[plane, 64:96] = jnp.where(lane < 32, turned[1], turned[3])
            target[plane, 96:] = jnp.where(
                (lane16 >= 32) & (lane16 < 96), turned[1][:16], pltpu.roll(turned[1][16:], 64, 1)
            )
            for dz in (-1, 1, 0):
                if plane != 4 or dz:
                    pairs(plane, dz).start()

    def quarter(x, first):
        out = x[:8]
        for m in range(1, 4):
            moved = pltpu.roll(x[8 * m : 8 * m + 8], L2 * m, 1)
            out = jnp.where(lane8 // L2 == (first + m) % 4, moved, out)
        return out

    def unquarter(q):
        parts = [q] + [pltpu.roll(q, LANES - L2 * m, 1) for m in range(1, 4)]
        return jnp.concatenate(parts, axis=0)

    def unhalf(h):
        return jnp.concatenate([h, pltpu.roll(h, 64, 1)], axis=0)

    def pairs(plane, dz):
        dx, dy = plane // 3 - 1, plane % 3 - 1
        source = (dsend, msend, usend)[dz + 1]
        target = (drecv, mrecv, urecv)[dz + 1]
        send = (d_send, m_send, u_send)[dz + 1]
        recv = (d_recv, m_recv, u_recv)[dz + 1]
        return remote(
            source.at[plane], target.at[plane], send.at[plane], recv.at[plane], peer(dx, dy, dz)
        )

    on = blocks[...]
    for i in range(WINDOW):
        spread1[i] = spread(image1[i * L2 : (i + 1) * L2, :], on)
    for plane in ORDER[::-1]:
        windows_of(plane)
    for i in range(WINDOW):
        cell = cell_at(i)
        x = times(spread1[i], cell)
        w[1, cell * L2 : (cell + 1) * L2, :] = both(x)

    @pl.loop(1, ITERS - 1)
    def _(n):
        now = lax.rem(n, 2)
        sweep(now, 1 - now)

    for planes in ((0, 1, 2), (3, 4, 5), (6, 7, 8)):
        last_sweep((ITERS - 1) % 2, planes)

    for offset in OFFSETS:
        halo(offset).wait_send()


    @pl.loop(0, 3)
    def _(n):
        for m in range(4):
            i = 4 * n + m
            turned = rnat[pl.ds(pl.multiple_of(i * LANES, LANES), LANES), :].T
            for j in range(4):
                out = None
                for s in range(DEPTH):
                    part = turned[s * L2 : (s + 1) * L2]
                    shift = (L2 * (s - j)) % LANES
                    part = pltpu.roll(part, shift, 1) if shift else part
                    out = part if out is None else jnp.where(lane // L2 == s, part, out)
                rb[i * 4 + j] = out

    for plane in ORDER:
        for dz in (-1, 0, 1):
            if plane != 4 or dz:
                pairs(plane, dz).wait_recv()
        u2, u1 = unhalf(urecv[plane, :16]), unquarter(urecv[plane, 16:])
        d2, d1 = unhalf(drecv[plane, :16]), unquarter(drecv[plane, 16:])
        outer, inner = mrecv[plane, 32:64], mrecv[plane, 64:96]
        rest = unhalf(mrecv[plane, 96:])
        got = [
            jnp.where(lane < 64, outer, d2),
            jnp.where(lane < 32, inner, jnp.where(lane < 96, rest, d1)),
            mrecv[plane, :32],
            jnp.where(lane < 32, u1, inner),
            jnp.where(lane < 64, u2, outer),
        ]
        for k in range(5):
            cell = WINDOW - 1 - (plane * 5 + k)
            prow[cell : cell + 1, :] = jnp.sum(got[k] * rb[cell], axis=0, keepdims=True)
        for dz in (-1, 0, 1):
            if plane != 4 or dz:
                pairs(plane, dz).wait_send()

    sr = lax.broadcasted_iota(jnp.int32, (8, LANES), 0)
    sc = lax.broadcasted_iota(jnp.int32, (8, LANES), 1)
    summed = jnp.where(sc // L2 == sr, 1.0, 0.0).astype(F32)
    sums = lax.dot_general(
        summed,
        prow[...],
        (((1,), (1,)), ((), ())),
        precision=lax.Precision.HIGHEST,
        preferred_element_type=F32,
    )
    pair_ref[...] = sums[:DEPTH, :WINDOW]


def finish(tau_ref, pair_ref, tau_out, pair_out, sem):
    copies = (
        pltpu.make_async_copy(tau_ref, tau_out, sem.at[0]),
        pltpu.make_async_copy(pair_ref, pair_out, sem.at[1]),
    )
    for copy in copies:
        copy.start()
    for copy in copies:
        copy.wait()


def body(t_matrix, structure, species, members, delta_table):
    vmem = pl.BlockSpec(memory_space=pltpu.VMEM)
    dma = pltpu.SemaphoreType.DMA
    tau, pair = pl.pallas_call(
        kernel,
        out_shape=(
            jax.ShapeDtypeStruct((DEPTH, L2 * L2), F32),
            jax.ShapeDtypeStruct((DEPTH, WINDOW), F32),
        ),
        in_specs=[pl.BlockSpec(memory_space=pltpu.HBM)] * 5,
        out_specs=(vmem, vmem),
        scratch_shapes=[
            pltpu.VMEM((DEPTH, L2 * L2), F32),
            pltpu.SMEM((DEPTH,), jnp.int32),
            pltpu.VMEM((DEPTH, WINDOW), jnp.int32),
            pltpu.VMEM((SPECIES, L2 * L2), F32),
            pltpu.VMEM((ROWS, ROWS), F32),
            pltpu.VMEM((ROWS, PADDED), BF16),
            pltpu.VMEM((ROWS, PADDED), BF16),
            pltpu.VMEM((2, PADDED, 2 * LANES), BF16),
            pltpu.VMEM((WINDOW, 2 * L2, LANES), BF16),
            pltpu.VMEM((9, L2, LANES), F32),
            pltpu.VMEM((9, L2 // 2, LANES), F32),
            pltpu.VMEM((9, L2 // 2, LANES), F32),
            pltpu.VMEM((L2 // 2, LANES), F32),
            pltpu.VMEM((L2 // 2, LANES), F32),
            pltpu.VMEM((48, LANES), F32),
            pltpu.VMEM((LANES, LANES), BF16),
            pltpu.VMEM((2 * LANES, 2 * LANES), BF16),
            pltpu.VMEM((L2, LANES), F32),
            pltpu.VMEM((ROWS, LANES), F32),
            pltpu.VMEM((WINDOW, LANES, 2 * LANES), BF16),
            pltpu.VMEM((PADDED, LANES), F32),
            pltpu.VMEM((48, L2, LANES), F32),
            pltpu.VMEM((48, LANES), F32),
            pltpu.VMEM((9, 112, LANES), F32),
            pltpu.VMEM((9, 24, LANES), F32),
            pltpu.VMEM((9, 24, LANES), F32),
            pltpu.VMEM((9, 112, LANES), F32),
            pltpu.VMEM((9, 24, LANES), F32),
            pltpu.VMEM((9, 24, LANES), F32),
        ]
        + [dma((4,))]
        + [dma((9,))] * 13,
        compiler_params=pltpu.CompilerParams(
            collective_id=0, has_side_effects=True, vmem_limit_bytes=50 << 20
        ),
    )(
        *(
            pltpu.with_memory_space_constraint(x, pltpu.HBM)
            for x in (
                t_matrix.reshape(DEPTH, L2 * L2),
                structure,
                species.reshape(DEPTH),
                members.reshape(DEPTH, WINDOW),
                delta_table,
            )
        )
    )
    anywhere = pl.BlockSpec(memory_space=pl.ANY)
    tau, pair = pl.pallas_call(
        finish,
        out_shape=(
            jax.ShapeDtypeStruct((DEPTH, L2 * L2), F32),
            jax.ShapeDtypeStruct((DEPTH, WINDOW), F32),
        ),
        in_specs=[anywhere] * 2,
        out_specs=(anywhere,) * 2,
        scratch_shapes=[dma((2,))],
        compiler_params=pltpu.CompilerParams(vmem_limit_bytes=16 << 20),
    )(tau, pair)
    return tau.reshape(1, 1, 1, DEPTH, L2 * L2), pair.reshape(1, 1, DEPTH, WINDOW)


def solution(mesh):
    placed = (
        P(None, "gx", "gy", "gz", None),
        P(),
        P("gx", "gy", "gz"),
        P("gx", "gy", "gz", None),
        P(),
    )
    return jax.shard_map(
        body,
        mesh=mesh,
        in_specs=placed,
        out_specs=(P(None, "gx", "gy", "gz", None), P("gx", "gy", "gz", None)),
        check_vma=False,
    )
```

```python
import jax
import jax.numpy as jnp
from jax import lax
from jax.experimental import pallas as pl
from jax.experimental.pallas import tpu as pltpu
from jax.sharding import PartitionSpec as P

L2 = 32
WINDOW = 45
ITERS = 4
SPECIES = 4
DEPTH = 4
LANES = DEPTH * L2
ROWS = WINDOW * L2
PADDED = 1536
CHUNK = ROWS // 3
CELLS = WINDOW // 3
CENTRE = WINDOW // 2
F32 = jnp.float32
BF16 = jnp.bfloat16
MESH = pl.DeviceIdType.MESH
ORDER = (0, 8, 2, 6, 3, 5, 1, 7, 4)
OFFSETS = sorted(
    [(x, y, z) for x in (-1, 0, 1) for y in (-1, 0, 1) for z in (-1, 0, 1) if x or y or z],
    key=lambda o: -(abs(o[0]) + abs(o[1]) + abs(o[2])),
)


def cell_at(position):
    return ORDER[position // 5] * 5 + position % 5


def split(x):
    high = x.astype(BF16)
    return high, (x - high.astype(F32)).astype(BF16)


def dot(a, b):
    return jnp.dot(a, b, preferred_element_type=F32)


def turned4(p):
    q = jnp.concatenate([p, p], axis=0)
    row = lax.broadcasted_iota(jnp.int32, (8, LANES), 0)
    block = lax.broadcasted_iota(jnp.int32, (8, LANES), 1) // L2
    out = q
    for d in range(1, 4):
        moved = pltpu.roll(pltpu.roll(q, L2 * d, 1), 8 - d, 0)
        out = jnp.where((block - row + 8) % 4 == d, moved, out)
    return out[:4]


def kernel(
    t_hbm,
    s_hbm,
    species_hbm,
    members_hbm,
    table_hbm,
    tau_ref,
    pair_ref,
    t_ref,
    species_ref,
    members_ref,
    table_ref,
    sf,
    sh,
    sl,
    w,
    tw,
    halo_c,
    halo_l,
    halo_r,
    pack_u,
    pack_d,
    mask,
    blocks,
    dbd,
    tc,
    image1,
    spread1,
    rnat,
    rb,
    prow,
    msend,
    usend,
    dsend,
    mrecv,
    urecv,
    drecv,
    in_sem,
    s_sem,
    hc_send,
    hl_send,
    hr_send,
    hc_recv,
    hl_recv,
    hr_recv,
    m_send,
    u_send,
    d_send,
    m_recv,
    u_recv,
    d_recv,
):
    gx, gy, gz = lax.axis_index("gx"), lax.axis_index("gy"), lax.axis_index("gz")
    nx, ny, nz = lax.axis_size("gx"), lax.axis_size("gy"), lax.axis_size("gz")

    xs = (lax.rem(gx + nx - 1, nx), gx, lax.rem(gx + 1, nx))
    ys = (lax.rem(gy + ny - 1, ny), gy, lax.rem(gy + 1, ny))
    zs = (lax.rem(gz + nz - 1, nz), gz, lax.rem(gz + 1, nz))

    def peer(dx, dy, dz):
        return (xs[dx + 1], ys[dy + 1], zs[dz + 1])

    inputs = [
        pltpu.make_async_copy(source, target, in_sem.at[i])
        for i, (source, target) in enumerate(
            (
                (t_hbm, t_ref),
                (species_hbm, species_ref),
                (members_hbm, members_ref),
                (table_hbm, table_ref),
            )
        )
    ]
    for copy in inputs:
        copy.start()

    barrier = pltpu.get_barrier_semaphore()
    for offset in OFFSETS:
        pl.semaphore_signal(barrier, inc=1, device_id=peer(*offset), device_id_type=MESH)

    def rows_copy(i):
        return pltpu.make_async_copy(
            s_hbm.at[0, pl.ds(ORDER[i] * 160, 160), :],
            sf.at[pl.ds(i * 160, 160), :],
            s_sem.at[i],
        )

    for i in range(9):
        rows_copy(i).start()

    lane = lax.broadcasted_iota(jnp.int32, (L2, LANES), 1)
    lane8 = lax.broadcasted_iota(jnp.int32, (8, LANES), 1)
    lane16 = lax.broadcasted_iota(jnp.int32, (L2 // 2, LANES), 1)
    inputs[0].wait()
    for k in range(8):
        tc[4 * k : 4 * k + 4, :] = turned4(t_ref[:, k * LANES : (k + 1) * LANES])
    t = tc[...]
    top, low = t[: L2 // 2], t[L2 // 2 :]
    pack_u[...] = jnp.where(lane16 < 64, pltpu.roll(top, 64, 1), low)
    pack_d[...] = jnp.where(lane16 < 64, top, pltpu.roll(low, 64, 1))
    halo_c[4] = t

    pl.semaphore_wait(barrier, 26)

    def remote(src, dst, send, recv, device):
        return pltpu.make_async_remote_copy(
            src_ref=src,
            dst_ref=dst,
            send_sem=send,
            recv_sem=recv,
            device_id=device,
            device_id_type=MESH,
        )

    def halo(offset):
        dx, dy, dz = offset
        plane = (dx + 1) * 3 + dy + 1
        slot = 8 - plane
        source = (pack_d, tc, pack_u)[dz + 1]
        target = (halo_r, halo_c, halo_l)[dz + 1]
        send = (hr_send, hc_send, hl_send)[dz + 1]
        recv = (hr_recv, hc_recv, hl_recv)[dz + 1]
        return remote(source, target.at[slot], send.at[plane], recv.at[slot], peer(*offset))

    for offset in OFFSETS:
        halo(offset).start()

    for copy in inputs[1:]:
        copy.wait()
    cells = lax.broadcasted_iota(jnp.int32, (48, WINDOW), 0)
    lane48 = lax.broadcasted_iota(jnp.int32, (48, LANES), 1)
    member = jnp.zeros((48, LANES), F32)
    for s in range(DEPTH):
        hit = jnp.where(members_ref[s : s + 1, :] == cells, 1.0, 0.0).astype(F32)
        some = jnp.max(hit, axis=1, keepdims=True)
        member = jnp.where(lane48 // L2 == s, some, member)
    mask[...] = member

    br = lax.broadcasted_iota(jnp.int32, (LANES, LANES), 0)
    bc = lax.broadcasted_iota(jnp.int32, (LANES, LANES), 1)
    blocks[...] = jnp.where(br // L2 == bc // L2, 1.0, 0.0).astype(BF16)

    deltas = jnp.concatenate(
        [turned4(table_ref[:, k * LANES : (k + 1) * LANES]) for k in range(8)], axis=0
    )
    code = jnp.zeros((L2, LANES), jnp.int32)
    for s in range(DEPTH):
        code = jnp.where(lane // L2 == s, s + 4 - species_ref[s], code)
    code = code % 4
    chosen = deltas
    for m in range(1, 4):
        chosen = jnp.where(code == m, pltpu.roll(deltas, L2 * m, 1), chosen)
    for s in range(DEPTH):
        dh, dl = split(jnp.where(lane // L2 == s, chosen, 0.0))
        rows = slice(s * L2, (s + 1) * L2)
        down = slice(LANES + s * L2, LANES + (s + 1) * L2)
        dbd[rows, :LANES] = dh
        dbd[rows, LANES:] = dl
        dbd[down, :LANES] = dh
        dbd[down, LANES:] = jnp.zeros((L2, LANES), BF16)

    w[:, 512:768, :] = jnp.zeros((2, 256, 2 * LANES), BF16)
    w[:, ROWS:, :] = jnp.zeros((2, PADDED - ROWS, 2 * LANES), BF16)
    rnat[ROWS:, :] = jnp.zeros((PADDED - ROWS, LANES), F32)
    prow[WINDOW:, :] = jnp.zeros((48 - WINDOW, LANES), F32)
    th, tl = split(t)
    w[0, CENTRE * L2 : (CENTRE + 1) * L2, :LANES] = th
    w[0, CENTRE * L2 : (CENTRE + 1) * L2, LANES:] = tl
    sh[:, ROWS:] = jnp.zeros((ROWS, PADDED - ROWS), BF16)
    sl[:, ROWS:] = jnp.zeros((ROWS, PADDED - ROWS), BF16)

    for i in range(3):
        for j in range(3):
            rows_copy(3 * i + j).wait()
        rows = pl.ds(i * CHUNK, CHUNK)
        high, rest = split(sf[rows, :])
        sh[rows, :ROWS] = high
        sl[rows, :ROWS] = rest

    wide = w[0, 512:768, :]
    a = dot(sh[:, 512:768], wide)
    b = dot(sl[:, 512:768], wide[:, :LANES])
    image1[...] = a[:, :LANES] + (a[:, LANES:] + b)

    def windows_of(plane):
        dx, dy = plane // 3 - 1, plane % 3 - 1
        for dz in (-1, 0, 1):
            if (dx, dy, dz) != (0, 0, 0):
                halo((-dx, -dy, -dz)).wait_recv()
        centre = halo_c[plane]
        up, down = halo_l[plane], halo_r[plane]
        left = jnp.concatenate([pltpu.roll(up, 64, 1), up], axis=0)
        right = jnp.concatenate([down, pltpu.roll(down, 64, 1)], axis=0)
        windows = [
            pltpu.roll(jnp.where(lane < 64, centre, left), 64, 1),
            pltpu.roll(jnp.where(lane < 96, centre, left), 32, 1),
            centre,
            pltpu.roll(jnp.where(lane < 32, right, centre), 96, 1),
            pltpu.roll(jnp.where(lane < 64, right, centre), 64, 1),
        ]
        for k in range(5):
            cell = plane * 5 + k
            th, tl = split(windows[k] * mask[cell : cell + 1, :])
            tw[cell, :L2] = th
            tw[cell, L2:] = tl

    def spread(image, on):
        ih, il = split(image)
        return jnp.concatenate(
            [
                jnp.concatenate([ih] * DEPTH, axis=0) * on,
                jnp.concatenate([il] * DEPTH, axis=0) * on,
            ],
            axis=1,
        )

    def blocks_times(image, cell, on):
        return times(spread(image, on), cell)

    def times(wide, cell):
        res = dot(tw[cell], wide)
        x = res[:L2, :LANES] + (res[:L2, LANES:] + res[L2:, :LANES])
        return x + tc[...] if cell == CENTRE else x

    def both(x):
        return jnp.concatenate(split(x), axis=1)

    def images(rows, now):
        wide = w[now]
        a = dot(sh[rows, :], wide)
        b = dot(sl[rows, :], wide[:, :LANES])
        return a[:, :LANES] + (a[:, LANES:] + b)

    def sweep(now, later):
        image = images(slice(0, ROWS), now)
        on = blocks[...]
        for i in range(WINDOW):
            cell = cell_at(i)
            x = blocks_times(image[i * L2 : (i + 1) * L2], cell, on)
            w[later, cell * L2 : (cell + 1) * L2, :] = both(x)

    def last_sweep(now, planes):
        start = planes[0] * 160
        size = len(planes) * 160
        image = images(slice(start, start + size), now)
        on = blocks[...]
        columns = []
        for i in range(size // L2):
            cell = cell_at(planes[0] * 5 + i)
            x = blocks_times(image[i * L2 : (i + 1) * L2], cell, on)
            if cell == CENTRE:
                for k in range(8):
                    tau_ref[:, k * LANES : (k + 1) * LANES] = turned4(x[4 * k : 4 * k + 4])
            columns.append(both(x))
        r2 = dot(jnp.concatenate(columns, axis=0), dbd[...])
        r = r2[:, :LANES] + r2[:, LANES:]
        for j, position in enumerate(planes):
            plane = ORDER[position]
            rnat[plane * 160 : (plane + 1) * 160, :] = r[j * 160 : (j + 1) * 160]
            turned = []
            for k in range(5):
                at = j * 160 + k * L2
                block = r[at : at + L2]
                turned.append(pltpu.roll(block, (L2 * (k - 2)) % LANES, 1) if k != 2 else block)
            usend[plane, :16] = jnp.where(
                lane16 < 64, turned[4][:16], pltpu.roll(turned[4][16:], 64, 1)
            )
            usend[plane, 16:] = quarter(turned[3], 0)
            dsend[plane, :16] = jnp.where(
                lane16 >= 64, turned[0][:16], pltpu.roll(turned[0][16:], 64, 1)
            )
            dsend[plane, 16:] = quarter(turned[1], 3)
            target = mrecv if plane == 4 else msend
            target[plane, :32] = turned[2]
            target[plane, 32:64] = jnp.where(lane >= 64, turned[4], turned[0])
            target[plane, 64:96] = jnp.where(lane < 32, turned[1], turned[3])
            target[plane, 96:] = jnp.where(
                (lane16 >= 32) & (lane16 < 96), turned[1][:16], pltpu.roll(turned[1][16:], 64, 1)
            )
            for dz in (-1, 1, 0):
                if plane != 4 or dz:
                    pairs(plane, dz).start()

    def quarter(x, first):
        out = x[:8]
        for m in range(1, 4):
            moved = pltpu.roll(x[8 * m : 8 * m + 8], L2 * m, 1)
            out = jnp.where(lane8 // L2 == (first + m) % 4, moved, out)
        return out

    def unquarter(q):
        parts = [q] + [pltpu.roll(q, LANES - L2 * m, 1) for m in range(1, 4)]
        return jnp.concatenate(parts, axis=0)

    def unhalf(h):
        return jnp.concatenate([h, pltpu.roll(h, 64, 1)], axis=0)

    def pairs(plane, dz):
        dx, dy = plane // 3 - 1, plane % 3 - 1
        source = (dsend, msend, usend)[dz + 1]
        target = (drecv, mrecv, urecv)[dz + 1]
        send = (d_send, m_send, u_send)[dz + 1]
        recv = (d_recv, m_recv, u_recv)[dz + 1]
        return remote(
            source.at[plane], target.at[plane], send.at[plane], recv.at[plane], peer(dx, dy, dz)
        )

    on = blocks[...]
    for i in range(WINDOW):
        spread1[i] = spread(image1[i * L2 : (i + 1) * L2, :], on)
    for plane in ORDER[::-1]:
        windows_of(plane)
    for i in range(WINDOW):
        cell = cell_at(i)
        x = times(spread1[i], cell)
        w[1, cell * L2 : (cell + 1) * L2, :] = both(x)

    @pl.loop(1, ITERS - 1)
    def _(n):
        now = lax.rem(n, 2)
        sweep(now, 1 - now)

    for planes in ((0, 1), (2, 3, 4, 5), (6, 7, 8)):
        last_sweep((ITERS - 1) % 2, planes)

    for offset in OFFSETS:
        halo(offset).wait_send()


    @pl.loop(0, 3)
    def _(n):
        for m in range(4):
            i = 4 * n + m
            turned = rnat[pl.ds(pl.multiple_of(i * LANES, LANES), LANES), :].T
            for j in range(4):
                out = None
                for s in range(DEPTH):
                    part = turned[s * L2 : (s + 1) * L2]
                    shift = (L2 * (s - j)) % LANES
                    part = pltpu.roll(part, shift, 1) if shift else part
                    out = part if out is None else jnp.where(lane // L2 == s, part, out)
                rb[i * 4 + j] = out

    for plane in ORDER:
        for dz in (-1, 0, 1):
            if plane != 4 or dz:
                pairs(plane, dz).wait_recv()
        u2, u1 = unhalf(urecv[plane, :16]), unquarter(urecv[plane, 16:])
        d2, d1 = unhalf(drecv[plane, :16]), unquarter(drecv[plane, 16:])
        outer, inner = mrecv[plane, 32:64], mrecv[plane, 64:96]
        rest = unhalf(mrecv[plane, 96:])
        got = [
            jnp.where(lane < 64, outer, d2),
            jnp.where(lane < 32, inner, jnp.where(lane < 96, rest, d1)),
            mrecv[plane, :32],
            jnp.where(lane < 32, u1, inner),
            jnp.where(lane < 64, u2, outer),
        ]
        for k in range(5):
            cell = WINDOW - 1 - (plane * 5 + k)
            prow[cell : cell + 1, :] = jnp.sum(got[k] * rb[cell], axis=0, keepdims=True)
        for dz in (-1, 0, 1):
            if plane != 4 or dz:
                pairs(plane, dz).wait_send()

    sr = lax.broadcasted_iota(jnp.int32, (8, LANES), 0)
    sc = lax.broadcasted_iota(jnp.int32, (8, LANES), 1)
    summed = jnp.where(sc // L2 == sr, 1.0, 0.0).astype(F32)
    sums = lax.dot_general(
        summed,
        prow[...],
        (((1,), (1,)), ((), ())),
        precision=lax.Precision.HIGHEST,
        preferred_element_type=F32,
    )
    pair_ref[...] = sums[:DEPTH, :WINDOW]


def finish(tau_ref, pair_ref, tau_out, pair_out, sem):
    copies = (
        pltpu.make_async_copy(tau_ref, tau_out, sem.at[0]),
        pltpu.make_async_copy(pair_ref, pair_out, sem.at[1]),
    )
    for copy in copies:
        copy.start()
    for copy in copies:
        copy.wait()


def body(t_matrix, structure, species, members, delta_table):
    vmem = pl.BlockSpec(memory_space=pltpu.VMEM)
    dma = pltpu.SemaphoreType.DMA
    tau, pair = pl.pallas_call(
        kernel,
        out_shape=(
            jax.ShapeDtypeStruct((DEPTH, L2 * L2), F32),
            jax.ShapeDtypeStruct((DEPTH, WINDOW), F32),
        ),
        in_specs=[pl.BlockSpec(memory_space=pltpu.HBM)] * 5,
        out_specs=(vmem, vmem),
        scratch_shapes=[
            pltpu.VMEM((DEPTH, L2 * L2), F32),
            pltpu.SMEM((DEPTH,), jnp.int32),
            pltpu.VMEM((DEPTH, WINDOW), jnp.int32),
            pltpu.VMEM((SPECIES, L2 * L2), F32),
            pltpu.VMEM((ROWS, ROWS), F32),
            pltpu.VMEM((ROWS, PADDED), BF16),
            pltpu.VMEM((ROWS, PADDED), BF16),
            pltpu.VMEM((2, PADDED, 2 * LANES), BF16),
            pltpu.VMEM((WINDOW, 2 * L2, LANES), BF16),
            pltpu.VMEM((9, L2, LANES), F32),
            pltpu.VMEM((9, L2 // 2, LANES), F32),
            pltpu.VMEM((9, L2 // 2, LANES), F32),
            pltpu.VMEM((L2 // 2, LANES), F32),
            pltpu.VMEM((L2 // 2, LANES), F32),
            pltpu.VMEM((48, LANES), F32),
            pltpu.VMEM((LANES, LANES), BF16),
            pltpu.VMEM((2 * LANES, 2 * LANES), BF16),
            pltpu.VMEM((L2, LANES), F32),
            pltpu.VMEM((ROWS, LANES), F32),
            pltpu.VMEM((WINDOW, LANES, 2 * LANES), BF16),
            pltpu.VMEM((PADDED, LANES), F32),
            pltpu.VMEM((48, L2, LANES), F32),
            pltpu.VMEM((48, LANES), F32),
            pltpu.VMEM((9, 112, LANES), F32),
            pltpu.VMEM((9, 24, LANES), F32),
            pltpu.VMEM((9, 24, LANES), F32),
            pltpu.VMEM((9, 112, LANES), F32),
            pltpu.VMEM((9, 24, LANES), F32),
            pltpu.VMEM((9, 24, LANES), F32),
        ]
        + [dma((4,))]
        + [dma((9,))] * 13,
        compiler_params=pltpu.CompilerParams(
            collective_id=0, has_side_effects=True, vmem_limit_bytes=50 << 20
        ),
    )(
        *(
            pltpu.with_memory_space_constraint(x, pltpu.HBM)
            for x in (
                t_matrix.reshape(DEPTH, L2 * L2),
                structure,
                species.reshape(DEPTH),
                members.reshape(DEPTH, WINDOW),
                delta_table,
            )
        )
    )
    anywhere = pl.BlockSpec(memory_space=pl.ANY)
    tau, pair = pl.pallas_call(
        finish,
        out_shape=(
            jax.ShapeDtypeStruct((DEPTH, L2 * L2), F32),
            jax.ShapeDtypeStruct((DEPTH, WINDOW), F32),
        ),
        in_specs=[anywhere] * 2,
        out_specs=(anywhere,) * 2,
        scratch_shapes=[dma((2,))],
        compiler_params=pltpu.CompilerParams(vmem_limit_bytes=16 << 20),
    )(tau, pair)
    return tau.reshape(1, 1, 1, DEPTH, L2 * L2), pair.reshape(1, 1, DEPTH, WINDOW)


def solution(mesh):
    placed = (
        P(None, "gx", "gy", "gz", None),
        P(),
        P("gx", "gy", "gz"),
        P("gx", "gy", "gz", None),
        P(),
    )
    return jax.shard_map(
        body,
        mesh=mesh,
        in_specs=placed,
        out_specs=(P(None, "gx", "gy", "gz", None), P("gx", "gy", "gz", None)),
        check_vma=False,
    )
```
